512 devices in a mesh: pipe: 16 (over y, core), seq: 32 (over x, z).
Axes of the slice: x: 4, y: 8, z: 8, core: 2. Of those that a mesh axis runs over, the one named last changes fastest.
Arguments:
- act_in: bfloat16 [16, 4096, 2048], P('pipe', 'seq'), may hold values from -20 to 20
- saved_in: bfloat16 [16, 4096, 2048], P('pipe', 'seq'), may hold values from -20 to 20
- grad_in: bfloat16 [16, 4096, 2048], P('pipe', 'seq'), may hold values from -18 to 18
- gain: float32 [16, 2048], P('pipe'), may hold values from 0.5 to 1.5
- weight: bfloat16 [16, 512, 4, 512], P('pipe', 'seq'), may hold values from -0.25 to 0.25
- left_blocks: bfloat16 [16, 64, 64, 64], P('pipe', 'seq'), may hold values from -0.75 to 0.75
- right_blocks: bfloat16 [16, 64, 64, 64], P('pipe', 'seq'), may hold values from -0.75 to 0.75
Outputs:
- handed_on: bfloat16 [16, 4096, 2048], P('pipe', 'seq')
- grad_handed: bfloat16 [16, 4096, 2048], P('pipe', 'seq')
- grad_weight: float32 [16, 512, 4, 512], P('pipe', 'seq')
- grad_gain: float32 [16, 2048], P('pipe')
- grad_left: float32 [16, 64, 64, 64], P('pipe', 'seq')
- grad_right: float32 [16, 64, 64, 64], P('pipe', 'seq')
The draws below stay inside these ranges and needn't reach their ends.
All inputs are finite; a program needn't handle non-finite values.
Results may differ from the reference program's by a relative error of at most 0.0076.
Values may be sent and summed in bfloat16 or wider, within the bound.
A program may use at most 64 MiB of HBM per device.

```python
import jax
import jax.numpy as jnp
from jax import lax

D = 2048
NB = 4
BD = 512
BLOCK = 64
TOKENS = 4096
SEQ_BLOCKS = 64
N_PIPE = 16


def activation_field(key):
    key_scale, key_base = jax.random.split(key, 2)
    shape = (N_PIPE, TOKENS, D)
    row_scale = jnp.exp(jax.random.uniform(key_scale, (N_PIPE, TOKENS, 1), jnp.float32, jnp.log(0.5), jnp.log(5.0)))
    values = jax.random.normal(key_base, shape, jnp.float32)
    values = jnp.clip(values, -4.0, 4.0)
    return (values * row_scale).astype(jnp.bfloat16)


def draw_act_in(key, part):
    return activation_field(jax.random.fold_in(key, 101))


def draw_saved_in(key, part):
    return activation_field(jax.random.fold_in(key, 202))


def draw_grad_in(key, part):
    key_scale, key_base = jax.random.split(jax.random.fold_in(key, 303), 2)
    shape = (N_PIPE, TOKENS, D)
    position = jnp.arange(TOKENS, dtype=jnp.float32).reshape(1, TOKENS, 1)
    trend = 1.0 + 2.0 * position / (TOKENS - 1)
    row_scale = jnp.exp(jax.random.uniform(key_scale, (N_PIPE, TOKENS, 1), jnp.float32, jnp.log(0.5), jnp.log(1.5))) * trend
    values = jax.random.normal(key_base, shape, jnp.float32)
    values = jnp.clip(values, -4.0, 4.0)
    return (values * row_scale).astype(jnp.bfloat16)


def steps_of(rng, extent, pieces, least, high):
    def one(dim, shards_of):
        draws = jax.random.uniform(jax.random.fold_in(jax.random.fold_in(rng, 6), dim), (shards_of,), jnp.float32, least / len(pieces), high / len(pieces))
        return jnp.repeat(jnp.exp(draws), extent[dim] // shards_of).reshape((-1,) + (1,) * (len(extent) - dim - 1))

    level = one(*pieces[0])
    for cut in pieces[1:]:
        level = level * one(*cut)
    return level


def gaussian(key, dims, scale, bound, cuts=(), kind=jnp.bfloat16):
    drawn = scale * jax.random.normal(key, dims, jnp.float32)
    if cuts:
        drawn = drawn * steps_of(key, dims, cuts, -0.22, 0.18)
    return jnp.clip(drawn, -bound, bound).astype(kind)


def setup_inputs(seed: int = 0) -> dict:
    keys = jax.random.split(jax.random.key(seed), 8)
    return {
        "act_in": draw_act_in(jax.random.fold_in(keys[7], 71), 0),
        "saved_in": draw_saved_in(jax.random.fold_in(keys[7], 71), 0),
        "grad_in": draw_grad_in(jax.random.fold_in(keys[7], 71), 0),
        "gain": jnp.clip(1.0 + 0.1 * jax.random.normal(keys[3], (N_PIPE, D), jnp.float32), 0.5, 1.5),
        "weight": gaussian(keys[4], (N_PIPE, BD, NB, BD), BD ** -0.5, 0.25, ((0, 16), (1, 32))),
        "left_blocks": gaussian(keys[5], (N_PIPE, SEQ_BLOCKS, BLOCK, BLOCK), BLOCK ** -0.5, 0.75, ((0, 16), (1, 32))),
        "right_blocks": gaussian(keys[6], (N_PIPE, BLOCK, SEQ_BLOCKS, SEQ_BLOCKS), SEQ_BLOCKS ** -0.5, 0.75, ((0, 16), (1, 32))),
    }


def normalize(rows, gain_row):
    widened = rows.astype(jnp.float32)
    inv_rms = lax.rsqrt(lax.optimization_barrier(jnp.mean(widened * widened, axis=-1, keepdims=True)) + 1e-06)
    normed = widened * inv_rms
    return (inv_rms, normed, (normed * gain_row).astype(jnp.bfloat16))

def section(operands):
    current, stored, upstream, gain_row, weight, left_factor, right_factor = operands
    tokens_all, model_width = current.shape
    nblocks = weight.shape[1]
    inner_width = weight.shape[2]
    groups = left_factor.shape[0]
    block_len = left_factor.shape[1]
    wide_weight = weight.astype(jnp.float32)
    left_wide = left_factor.astype(jnp.float32)
    right_wide = right_factor.astype(jnp.float32)

    def project_in(normin):
        split_rows = normin.reshape(tokens_all, nblocks, inner_width).astype(jnp.float32)
        proj = jnp.einsum('tki,ikj->tkj', split_rows, wide_weight).astype(jnp.bfloat16)
        return proj.reshape(groups, block_len, model_width)

    def first_factor(proj):
        return jnp.einsum('abc,acd->abd', left_wide, proj.astype(jnp.float32)).astype(jnp.bfloat16)

    def second_factor(first_mix):
        return jnp.einsum('bxy,ybd->xbd', right_wide, first_mix.astype(jnp.float32)).astype(jnp.bfloat16)
    cur_scale, cur_norm, cur_in = normalize(current, gain_row)
    sto_scale, sto_norm, sto_in = normalize(stored, gain_row)
    cur_proj = project_in(cur_in)
    cur_mix = second_factor(first_factor(cur_proj))
    output = (current.astype(jnp.float32) + cur_proj.reshape(tokens_all, model_width).astype(jnp.float32) * cur_mix.reshape(tokens_all, model_width).astype(jnp.float32)).astype(jnp.bfloat16)
    sto_proj = project_in(sto_in)
    sto_first = first_factor(sto_proj)
    sto_mix = second_factor(sto_first)
    upstream_g = upstream.reshape(groups, block_len, model_width).astype(jnp.float32)
    adjoint_mix = (upstream_g * sto_proj.astype(jnp.float32)).astype(jnp.bfloat16)
    adjoint_first = jnp.einsum('bxy,xbd->ybd', right_wide, adjoint_mix.astype(jnp.float32)).astype(jnp.bfloat16)
    right_grad = jnp.einsum('xbd,ybd->bxy', adjoint_mix.astype(jnp.float32), sto_first.astype(jnp.float32))
    local_grad = upstream_g * sto_mix.astype(jnp.float32) + jnp.einsum('abc,abd->acd', left_wide, adjoint_first.astype(jnp.float32))
    proj_grad = local_grad.astype(jnp.bfloat16).reshape(tokens_all, nblocks, inner_width).astype(jnp.float32)
    left_grad = jnp.einsum('abd,acd->abc', adjoint_first.astype(jnp.float32), sto_proj.astype(jnp.float32))
    normed_grad = jnp.einsum('tkj,ikj->tki', proj_grad, wide_weight).reshape(tokens_all, model_width)
    sto_split = sto_in.reshape(tokens_all, nblocks, inner_width).astype(jnp.float32)
    weight_grad = jnp.einsum('tki,tkj->ikj', sto_split, proj_grad)
    gain_grad = lax.optimization_barrier(jnp.sum(normed_grad * sto_norm, axis=0))
    scaled = normed_grad * gain_row
    input_grad = (upstream.astype(jnp.float32) + sto_scale * (scaled - sto_norm * lax.optimization_barrier(jnp.mean(scaled * sto_norm, axis=-1, keepdims=True)))).astype(jnp.bfloat16)
    return (output, input_grad, weight_grad, gain_grad, left_grad, right_grad)

def reference(act_in, saved_in, grad_in, gain, weight, left_blocks, right_blocks):
    results = lax.map(section, (act_in, saved_in, grad_in, gain, weight, left_blocks, right_blocks))
    handed_on = jnp.roll(results[0], 1, axis=0)
    grad_handed = jnp.roll(results[1], -1, axis=0)
    return (handed_on, grad_handed, results[2], results[3], results[4], results[5])
```

```python
import functools

import jax
import jax.numpy as jnp
from jax import lax
from jax.experimental import pallas as pl
from jax.experimental.pallas import tpu as pltpu
from jax.sharding import PartitionSpec as P

MESH = pl.DeviceIdType.MESH
F32 = jnp.float32
BF16 = jnp.bfloat16

KINDS = (
    "w", "sto", "left", "right", "stat", "grad", "act", "weight", "fs", "am", "fc", "ms", "af", "mc",
    "gw", "gg", "gr", "gl", "msum", "gwx", "ggx", "out", "gx",
)
SEM = {name: i for i, name in enumerate(KINDS)}


def dot(a, b):
    return lax.dot_general(a, b, (((1,), (0,)), ((), ())), preferred_element_type=F32)


def dot_t(a, b):
    return lax.dot_general(a, b, (((1,), (1,)), ((), ())), preferred_element_type=F32)


def kernel(
    n_pipe,
    act, sto, grd, gain, w, left, right,
    handed, gradh, gw_out, gg_out, gl_out, gr_out,
    xs, xg, xc, lg, rg, wk, wfull, st, stg, inv_s,
    ni_s, ni_c, ni_t, tmp, tmp2, q_m, q_t, s_t, l_m, l_t, r_m, r_t, p_s, p_c,
    fs, am, fc, fsr, amr, fcr, ms, af, mc, msr, afr, mcr,
    ap, an, gws, gwr, gwx, ggs, ggr, ggx, ggxr, msum, msumr, glp, glr, grp, grr, outb, gxb,
    send_sem, recv_sem,
):
    pipe = lax.axis_index("pipe")
    seq = lax.axis_index("seq")
    k = lax.div(seq, 8)
    g = lax.rem(seq, 8)
    nxt = lax.rem(pipe + 1, n_pipe)
    prv = lax.rem(pipe + n_pipe - 1, n_pipe)

    k_peers = [lax.rem(k + d, 4) for d in (2, 1, 3)]
    g_peers = [lax.rem(g + d, 8) for d in (4, 5, 3, 6, 2, 7, 1)]

    def dev_k(j):
        return (pipe, j * 8 + g)

    def dev_g(j):
        return (pipe, k * 8 + j)

    def send(kind, src, dst, dev):
        pltpu.make_async_remote_copy(
            src_ref=src, dst_ref=dst, send_sem=send_sem.at[SEM[kind]], recv_sem=recv_sem.at[SEM[kind]],
            device_id=dev, device_id_type=MESH,
        ).start()

    def wait(sem, kind, ref):
        pltpu.make_async_copy(ref, ref, sem.at[SEM[kind]]).wait()

    def arrived(kind, ref):
        wait(recv_sem, kind, ref)

    barrier = pltpu.get_barrier_semaphore()
    for j in k_peers:
        pl.semaphore_signal(barrier, inc=1, device_id=dev_k(j), device_id_type=MESH)
    for j in g_peers:
        pl.semaphore_signal(barrier, inc=1, device_id=dev_g(j), device_id_type=MESH)
    for q in (nxt, prv):
        for j in range(4):
            pl.semaphore_signal(barrier, inc=1, device_id=(q, j * 8 + g), device_id_type=MESH)
    pl.semaphore_wait(barrier, 18)

    def cols(j):
        return pl.ds(pl.multiple_of(j * 512, 512), 512)

    for j in k_peers:
        send("w", w.at[j], wk.at[k], dev_k(j))
    for j in k_peers:
        send("sto", sto.at[:, cols(j)], xs.at[k], dev_k(j))
        send("left", left, lg.at[k], dev_k(j))
        send("right", right, rg.at[k], dev_k(j))
    wk[k] = w[k]
    xs[k] = sto[:, cols(k)]

    def inv_row(x_ref):
        x = x_ref[...].astype(F32)
        inv = lax.rsqrt(jnp.sum(x * x, axis=1, keepdims=True) * (1.0 / 2048) + 1e-06)
        return jnp.transpose(jnp.broadcast_to(inv, (128, 128)))[0:8]

    st[0:8, :] = inv_row(sto)
    st[8:16, :] = inv_row(act)
    arrived("w", wk.at[pl.ds(0, 3)])
    for j in g_peers:
        send("weight", wk, wfull.at[:, g], dev_g(j))
    for j in k_peers:
        send("stat", st, stg.at[k], dev_k(j))
    for j in k_peers:
        send("grad", grd.at[:, cols(j)], xg.at[k], dev_k(j))
    for j in k_peers:
        send("act", act.at[:, cols(j)], xc.at[k], dev_k(j))
    wfull[:, g] = wk[...]
    stg[k] = st[...]
    xg[k] = grd[:, cols(k)]
    xc[k] = act[:, cols(k)]
    lg[k] = left[...]
    rg[k] = right[...]

    def pick_q(r):
        return 64 * ((r >> 3) & 7) + 16 * ((r & 7) >> 1) + 2 * (r >> 6) + (r & 1)

    def pick_s(r):
        return 64 * (r & 7) + 16 * ((r >> 4) & 3) + 2 * (r >> 6) + ((r >> 3) & 1)

    def hot(cond):
        return jnp.where(cond, 1.0, 0.0).astype(BF16)

    def rows(t, n=128):
        return pl.ds(pl.multiple_of(t * n, n), n)

    col = lax.broadcasted_iota(jnp.int32, (128, 512), 1)

    @pl.loop(0, 4)
    def _(t):
        row = lax.broadcasted_iota(jnp.int32, (128, 512), 0) + t * 128
        q_m[rows(t), :] = hot(col == pick_q(row))
        q_t[rows(t), :] = hot(row == pick_q(col))
        s_t[rows(t), :] = hot(row == pick_s(col))

    erow = lax.broadcasted_iota(jnp.int32, (64, 512), 0)
    ecol = lax.broadcasted_iota(jnp.int32, (64, 512), 1)

    arrived("left", lg.at[pl.ds(0, 3)])
    rep_c = hot(erow == (ecol & 63))

    @pl.loop(0, 4)
    def _(t):
        row = lax.broadcasted_iota(jnp.int32, (128, 512), 0) + t * 128
        wide = dot(lg[t].reshape(128, 64), rep_c)
        tmp[rows(t), :] = jnp.where((row >> 6) == (col >> 6), wide, 0.0).astype(BF16)

    @pl.loop(0, 2)
    def _(t):
        l_m[rows(t, 256), :] = dot(q_m[rows(t, 256), :], tmp[...]).astype(BF16)

    arrived("right", rg.at[pl.ds(0, 3)])
    rep_e = hot(erow == (pick_s(ecol) & 63))

    @pl.loop(0, 4)
    def _(t):
        row = lax.broadcasted_iota(jnp.int32, (128, 512), 0) + t * 128
        wide = dot(rg[t].reshape(128, 64), rep_e)
        tmp[rows(t), :] = jnp.where((row >> 6) == (col & 7), wide, 0.0).astype(BF16)

    @pl.loop(0, 4)
    def _(t):
        row = lax.broadcasted_iota(jnp.int32, (128, 512), 0) + t * 128
        r_m[rows(t), :] = dot(hot(col == pick_s(row)), tmp[...]).astype(BF16)

    def transposed(dst, src):
        for t in range(4):
            dst[:, t * 128:(t + 1) * 128] = jnp.transpose(src[t * 128:(t + 1) * 128, :].astype(F32)).astype(BF16)

    transposed(l_t, l_m)
    transposed(r_t, r_m)

    gain_k = gain[0:1, cols(k)]

    def column(row8):
        return jnp.transpose(jnp.broadcast_to(row8[0:1, :], (128, 128)))

    arrived("sto", xs.at[pl.ds(0, 3)])
    arrived("stat", stg.at[pl.ds(0, 3)])

    @pl.loop(0, 4)
    def _(t):
        inv = column(stg[t, 0:8, :])
        inv_s[t] = inv
        normed = xs[t].astype(F32) * inv[:, 0:1]
        ni_s[rows(t), :] = (normed * gain_k).astype(BF16)

    arrived("weight", wfull.at[:, pl.ds(0, 7)])

    def weight_block():
        return wfull[...].reshape(512, 512)

    def matmul(dst, a, b):
        @pl.loop(0, 2)
        def _(t):
            dst[rows(t, 256), :] = dot(a[rows(t, 256), :], b()).astype(dst.dtype)

    def matmul8(dst, a, b):
        @pl.loop(0, 2)
        def _(t):
            dst[pl.ds(t * 4, 4)] = dot(a[rows(t, 256), :], b()).astype(BF16).reshape(4, 64, 512)

    def scatter8(kind, src, dst):
        for j in g_peers:
            send(kind, src.at[j], dst.at[g], dev_g(j))
        dst[g] = src[g]

    def flat(ref):
        return lambda: ref[...].reshape(512, 512)

    def whole(ref):
        return lambda: ref[...]

    matmul(p_s, ni_s, weight_block)
    matmul8(fs, l_m, whole(p_s))
    scatter8("fs", fs, fsr)

    arrived("grad", xg.at[pl.ds(0, 3)])

    @pl.loop(0, 4)
    def _(t):
        tmp[rows(t), :] = (xg[t].astype(F32) * p_s[rows(t), :].astype(F32)).astype(BF16)

    matmul8(am, q_m, whole(tmp))
    scatter8("am", am, amr)

    arrived("act", xc.at[pl.ds(0, 3)])

    @pl.loop(0, 4)
    def _(t):
        inv = column(stg[t, 8:16, :])
        normed = xc[t].astype(F32) * inv[:, 0:1]
        ni_c[rows(t), :] = (normed * gain_k).astype(BF16)

    matmul(p_c, ni_c, weight_block)
    matmul8(fc, l_m, whole(p_c))
    scatter8("fc", fc, fcr)
    transposed(ni_t, ni_s)

    arrived("fs", fsr.at[pl.ds(0, 7)])
    matmul8(ms, r_m, flat(fsr))
    scatter8("ms", ms, msr)
    arrived("am", amr.at[pl.ds(0, 7)])
    matmul8(af, r_t, flat(amr))
    scatter8("af", af, afr)
    arrived("fc", fcr.at[pl.ds(0, 7)])
    matmul8(mc, r_m, flat(fcr))
    scatter8("mc", mc, mcr)

    matmul(tmp, s_t, flat(amr))
    matmul(tmp2, s_t, flat(fsr))

    @pl.loop(0, 8)
    def _(t):
        grp[t] = dot_t(tmp[rows(t, 64), :], tmp2[rows(t, 64), :])

    for j in k_peers:
        send("gr", grp.at[pl.ds(2 * j, 2)], grr.at[k], dev_k(j))
    grr[k] = grp[pl.ds(2 * k, 2)]

    arrived("ms", msr.at[pl.ds(0, 7)])
    arrived("af", afr.at[pl.ds(0, 7)])

    @pl.loop(0, 4)
    def _(t):
        mixed = dot(q_t[rows(t), :], msr[...].reshape(512, 512))
        through = dot(l_t[rows(t), :], afr[...].reshape(512, 512))
        adj = (xg[t].astype(F32) * mixed + through).astype(BF16)
        ap[rows(t), :] = adj
        part = jnp.sum(adj.astype(F32) * p_s[rows(t), :].astype(F32), axis=1, keepdims=True)
        msum[t] = jnp.transpose(jnp.broadcast_to(part, (128, 128)))[0:8]

    for j in k_peers:
        send("msum", msum, msumr.at[k], dev_k(j))
    msumr[k] = msum[...]

    @pl.loop(0, 4)
    def _(t):
        gws[t] = dot(ni_t[rows(t), :], ap[...]).astype(BF16).reshape(8, 16, 512)

    for j in g_peers:
        send("gw", gws.at[:, j], gwr.at[g], dev_g(j))
    gwr[g] = gws[:, g]

    ggs[...] = jnp.zeros((8, 512), F32)

    @pl.loop(0, 4)
    def _(t):
        adj_norm = dot_t(ap[rows(t), :], weight_block())
        an[rows(t), :] = adj_norm
        normed = xs[t].astype(F32) * inv_s[t, :, 0:1]
        ggs[...] += jnp.sum((adj_norm * normed).reshape(16, 8, 512), axis=0)

    for j in g_peers:
        send("gg", ggs, ggr.at[g], dev_g(j))
    ggr[g] = ggs[...]

    arrived("msum", msumr.at[pl.ds(0, 3)])

    @pl.loop(0, 4)
    def _(t):
        total = msumr[0, t] + msumr[1, t] + msumr[2, t] + msumr[3, t]
        mean = column(total)[:, 0:1] * (1.0 / 2048)
        inv = inv_s[t, :, 0:1]
        normed = xs[t].astype(F32) * inv
        scaled = an[rows(t), :] * gain_k
        gxb[t] = (xg[t].astype(F32) + inv * (scaled - normed * mean)).astype(BF16)

    for j in [k] + k_peers:
        send("gx", gxb.at[j], gradh.at[:, cols(k)], (prv, j * 8 + g))

    matmul(tmp, q_t, flat(afr))

    @pl.loop(0, 8)
    def _(t):
        glp[t] = dot_t(tmp[rows(t, 64), :], p_s[rows(t, 64), :])

    for j in k_peers:
        send("gl", glp.at[pl.ds(2 * j, 2)], glr.at[k], dev_k(j))
    glr[k] = glp[pl.ds(2 * k, 2)]

    arrived("mc", mcr.at[pl.ds(0, 7)])

    @pl.loop(0, 4)
    def _(t):
        mixed = dot(q_t[rows(t), :], mcr[...].reshape(512, 512))
        outb[t] = (xc[t].astype(F32) + p_c[rows(t), :].astype(F32) * mixed).astype(BF16)

    for j in [k] + k_peers:
        send("out", outb.at[j], handed.at[:, cols(k)], (nxt, j * 8 + g))

    arrived("gg", ggr.at[pl.ds(0, 7)])
    summed = ggr[0]
    for j in range(1, 8):
        summed = summed + ggr[j]
    ggx[...] = jnp.broadcast_to(jnp.sum(summed, axis=0, keepdims=True), (8, 512))
    for j in k_peers:
        send("ggx", ggx, ggxr.at[k], dev_k(j))
    ggxr[k] = ggx[...]

    arrived("gr", grr.at[pl.ds(0, 3)])
    gr_out[...] = grr[0] + grr[1] + grr[2] + grr[3]
    arrived("gl", glr.at[pl.ds(0, 3)])
    gl_out[...] = glr[0] + glr[1] + glr[2] + glr[3]

    arrived("gw", gwr.at[pl.ds(0, 7)])
    for t in range(4):
        acc = gwr[0, t].astype(F32)
        for j in range(1, 8):
            acc = acc + gwr[j, t].astype(F32)
        gwx[t] = acc
    for j in k_peers:
        send("gwx", gwx.at[j], gw_out.at[k], dev_k(j))
    gw_out[k] = gwx[k]

    arrived("ggx", ggxr.at[pl.ds(0, 3)])
    for j in range(4):
        gg_out[0:1, j * 512:(j + 1) * 512] = ggxr[j, 0:1, :]
    arrived("gwx", gw_out.at[pl.ds(0, 3)])
    arrived("gx", gradh)
    arrived("out", handed)

    for kind, ref in (
        ("w", wk.at[pl.ds(0, 3)]),
        ("sto", xs.at[pl.ds(0, 3)]),
        ("left", lg.at[pl.ds(0, 3)]),
        ("right", rg.at[pl.ds(0, 3)]),
        ("stat", stg.at[pl.ds(0, 3)]),
        ("grad", xg.at[pl.ds(0, 3)]),
        ("act", xc.at[pl.ds(0, 3)]),
        ("weight", wfull.at[:, pl.ds(0, 7)]),
        ("fs", fsr.at[pl.ds(0, 7)]),
        ("am", amr.at[pl.ds(0, 7)]),
        ("fc", fcr.at[pl.ds(0, 7)]),
        ("ms", msr.at[pl.ds(0, 7)]),
        ("af", afr.at[pl.ds(0, 7)]),
        ("mc", mcr.at[pl.ds(0, 7)]),
        ("gw", gwr.at[pl.ds(0, 7)]),
        ("gg", ggr.at[pl.ds(0, 7)]),
        ("gr", grr.at[pl.ds(0, 3)]),
        ("gl", glr.at[pl.ds(0, 3)]),
        ("msum", msumr.at[pl.ds(0, 3)]),
        ("gwx", gw_out.at[pl.ds(0, 3)]),
        ("ggx", ggxr.at[pl.ds(0, 3)]),
        ("out", outb),
        ("gx", gxb),
    ):
        wait(send_sem, kind, ref)


def section(n_pipe, act, sto, grd, gain, w, left, right):
    vmem = pl.BlockSpec(memory_space=pltpu.VMEM)
    hbm = pl.BlockSpec(memory_space=pl.ANY)
    big = pltpu.VMEM((512, 512), BF16)
    parts = pltpu.VMEM((8, 64, 512), BF16)
    tokens = pltpu.VMEM((4, 128, 512), BF16)
    factor = pltpu.VMEM((4, 2, 64, 64), BF16)
    scratch = (
        [tokens] * 3
        + [factor] * 2
        + [pltpu.VMEM((4, 16, 512), BF16), pltpu.VMEM((4, 8, 16, 512), BF16)]
        + [pltpu.VMEM((16, 128), F32), pltpu.VMEM((4, 16, 128), F32), pltpu.VMEM((4, 128, 128), F32)]
        + [big] * 14
        + [parts] * 12
        + [big, pltpu.VMEM((512, 512), F32)]
        + [pltpu.VMEM((4, 8, 16, 512), BF16), pltpu.VMEM((8, 4, 16, 512), BF16), pltpu.VMEM((4, 16, 512), F32)]
        + [pltpu.VMEM((8, 512), F32), pltpu.VMEM((8, 8, 512), F32), pltpu.VMEM((8, 512), F32), pltpu.VMEM((4, 8, 512), F32)]
        + [pltpu.VMEM((4, 8, 128), F32), pltpu.VMEM((4, 4, 8, 128), F32)]
        + [pltpu.VMEM((8, 64, 64), F32), pltpu.VMEM((4, 2, 64, 64), F32)] * 2
        + [tokens] * 2
        + [pltpu.SemaphoreType.DMA((len(KINDS),)), pltpu.SemaphoreType.DMA((len(KINDS),))]
    )
    return pl.pallas_call(
        functools.partial(kernel, n_pipe),
        out_shape=(
            jax.ShapeDtypeStruct((128, 2048), BF16),
            jax.ShapeDtypeStruct((128, 2048), BF16),
            jax.ShapeDtypeStruct((4, 16, 512), F32),
            jax.ShapeDtypeStruct((1, 2048), F32),
            jax.ShapeDtypeStruct((2, 64, 64), F32),
            jax.ShapeDtypeStruct((2, 64, 64), F32),
        ),
        in_specs=[vmem] * 7,
        out_specs=(hbm, hbm, vmem, vmem, vmem, vmem),
        scratch_shapes=scratch,
        compiler_params=pltpu.CompilerParams(
            collective_id=0, has_side_effects=True, vmem_limit_bytes=58 * 1024 * 1024
        ),
    )(act, sto, grd, gain, w, left, right)


def shards(n_pipe, act_in, saved_in, grad_in, gain, weight, left_blocks, right_blocks):
    w = jnp.transpose(weight[0], (1, 0, 2))
    handed, gradh, gw, gg, gl, gr = section(
        n_pipe, act_in[0], saved_in[0], grad_in[0], gain, w, left_blocks[0], right_blocks[0]
    )
    return (handed[None], gradh[None], jnp.transpose(gw, (1, 0, 2))[None], gg, gl[None], gr[None])


def solution(mesh):
    return jax.shard_map(
        functools.partial(shards, mesh.shape["pipe"]),
        mesh=mesh,
        in_specs=(
            P("pipe", "seq", None),
            P("pipe", "seq", None),
            P("pipe", "seq", None),
            P("pipe", None),
            P("pipe", "seq", None, None),
            P("pipe", "seq", None, None),
            P("pipe", "seq", None, None),
        ),
        out_specs=(
            P("pipe", "seq", None),
            P("pipe", "seq", None),
            P("pipe", "seq", None, None),
            P("pipe", None),
            P("pipe", "seq", None, None),
            P("pipe", "seq", None, None),
        ),
        check_vma=False,
    )
```

```python
import functools

import jax
import jax.numpy as jnp
from jax import lax
from jax.experimental import pallas as pl
from jax.experimental.pallas import tpu as pltpu
from jax.sharding import PartitionSpec as P

MESH = pl.DeviceIdType.MESH
F32 = jnp.float32
BF16 = jnp.bfloat16

KINDS = (
    "w", "gain", "sto", "left", "right", "stat", "grad", "act", "weight", "fs", "am", "fc", "ms", "af", "mc",
    "gw", "gg", "gr", "gl", "msum", "gwx", "ggx", "out", "gx",
)
SEM = {name: i for i, name in enumerate(KINDS)}


def dot(a, b):
    return lax.dot_general(a, b, (((1,), (0,)), ((), ())), preferred_element_type=F32)


def dot_t(a, b):
    return lax.dot_general(a, b, (((1,), (1,)), ((), ())), preferred_element_type=F32)


def kernel(
    n_pipe,
    act, sto, grd, gain, w, left, right,
    handed, gradh, gw_out, gg_out, gl_out, gr_out,
    act_v, sto_v, w4, lpk, rpk,
    xs, xg, xc, lg, rg, wk, wfull, wnat, gn, st, stg, inv_s,
    ni_s, ni_c, ni_t, tmp, tmp2, q_m, q_t, s_t, l_m, l_t, r_m, r_t, p_s, p_c,
    fs, am, fc, fsr, amr, fcr, ms, af, mc, msr, afr, mcr,
    ap, an, gws, gwr, gwx, ggs, ggr, ggx, msum, msumr, glp, grp, outb, gxb,
    send_sem, recv_sem, load_sem,
):
    load_act = pltpu.make_async_copy(act, act_v, load_sem.at[0])
    load_sto = pltpu.make_async_copy(sto, sto_v, load_sem.at[1])
    load_act.start()
    load_sto.start()

    pipe = lax.axis_index("pipe")
    seq = lax.axis_index("seq")
    core = lax.rem(pipe, 2)
    chip = pipe - core
    x = lax.div(seq, 8)
    z = lax.rem(seq, 8)
    side = lax.rem(z, 2)
    k = lax.div(z, 2)
    half = 1 - core
    g = 2 * x + half
    job = chip + side

    def ring(p):
        return lax.rem(p + n_pipe, n_pipe)

    turn = [lax.rem(k + d, 4) for d in (2, 1, 3, 0)]

    def worker_of(section, j):
        odd = lax.rem(section, 2)
        return (section - odd + 1 - side, 8 * x + 2 * j + odd)

    def owner_in(section, j):
        return (section, 8 * x + 2 * j + half)

    k_peers = [lax.rem(k + d, 4) for d in (2, 1, 3)]
    g_peers = [lax.rem(g + d, 8) for d in (4, 5, 3, 6, 2, 7, 1)]

    def dev_k(j):
        return (pipe, 8 * x + 2 * j + side)

    def dev_g(j):
        return (chip + 1 - lax.rem(j, 2), 8 * lax.div(j, 2) + z)

    def send(kind, src, dst, dev):
        pltpu.make_async_remote_copy(
            src_ref=src, dst_ref=dst, send_sem=send_sem.at[SEM[kind]], recv_sem=recv_sem.at[SEM[kind]],
            device_id=dev, device_id_type=MESH,
        ).start()

    def wait(sem, kind, ref):
        pltpu.make_async_copy(ref, ref, sem.at[SEM[kind]]).wait()

    def arrived(kind, ref):
        wait(recv_sem, kind, ref)

    met = [dev_k(j) for j in k_peers] + [dev_g(j) for j in g_peers]
    for d in (-1, 0, 1):
        met += [owner_in(ring(job + d), j) for j in range(4)]
        met += [worker_of(ring(pipe + d), j) for j in range(4)]
    barrier = pltpu.get_barrier_semaphore()
    for dev in met:
        pl.semaphore_signal(barrier, inc=1, device_id=dev, device_id_type=MESH)
    for j in range(4):
        w4[j] = w[:, j, :]
    for src, dst in ((left, lpk), (right, rpk)):
        dst[:, 0:64] = src[0]
        dst[:, 64:128] = src[1]
    def inv_row(x_ref):
        v = x_ref[...].astype(F32)
        inv = lax.rsqrt(jnp.sum(v * v, axis=1, keepdims=True) * (1.0 / 2048) + 1e-06)
        return jnp.transpose(jnp.broadcast_to(inv, (128, 128)))[0:8]

    load_act.wait()
    st[0:8, :] = inv_row(act_v)
    load_sto.wait()
    st[8:16, :] = inv_row(sto_v)
    pl.semaphore_wait(barrier, len(met))

    def cols(j):
        if isinstance(j, int):
            return pl.ds(j * 512, 512)
        return pl.ds(pl.multiple_of(j * 512, 512), 512)

    def send_out(kind, src, dst, to):
        for j in turn[:3]:
            send(kind, src.at[j], dst.at[:, cols(k)], owner_in(to, j))

        @pl.when(to == pipe)
        def _():
            pltpu.make_async_copy(src.at[k], dst.at[:, cols(k)], recv_sem.at[SEM[kind]]).start()

        @pl.when(to != pipe)
        def _():
            send(kind, src.at[k], dst.at[:, cols(k)], owner_in(to, k))

    def sent_out(kind, src, to):
        @pl.when(to == pipe)
        def _():
            wait(send_sem, kind, src.at[pl.ds(0, 3)])

        @pl.when(to != pipe)
        def _():
            wait(send_sem, kind, src)

    for j in turn:
        send("w", w4.at[j], wk.at[k], worker_of(pipe, j))
    for j in turn:
        send("left", lpk, lg.at[k], worker_of(pipe, j))
        send("gain", gain.at[:, cols(j)], gn.at[k], worker_of(pipe, j))
        send("stat", st, stg.at[k], worker_of(pipe, j))
    for j in turn:
        send("act", act.at[:, cols(j)], xc.at[k], worker_of(pipe, j))
    for j in turn:
        send("right", rpk, rg.at[k], worker_of(pipe, j))
    for j in turn:
        send("sto", sto.at[:, cols(j)], xs.at[k], worker_of(pipe, j))
    for j in turn:
        send("grad", grd.at[:, cols(j)], xg.at[k], worker_of(pipe, j))

    def nat(n, l):
        return 16 * (n >> 1) + 4 * (l >> 1) + 2 * (n & 1) + (l & 1)

    def pick_q(r):
        return 64 * ((r >> 3) & 7) + nat(r >> 6, r & 7)

    def pick_s(r):
        return 64 * (r & 7) + nat(r >> 6, (r >> 3) & 7)

    def hot(cond):
        return jnp.where(cond, 1.0, 0.0).astype(BF16)

    def rows(t, n=128):
        return pl.ds(pl.multiple_of(t * n, n), n)

    col = lax.broadcasted_iota(jnp.int32, (128, 512), 1)
    row0 = lax.broadcasted_iota(jnp.int32, (128, 512), 0)

    arrived("w", wk)
    for j in g_peers:
        send("weight", wk, wfull.at[g], dev_g(j))
    wfull[g] = wk[...]

    @pl.loop(0, 4)
    def _(t):
        row = row0 + t * 128
        q_m[rows(t), :] = hot(col == pick_q(row))
        q_t[rows(t), :] = hot(row == pick_q(col))
        s_t[rows(t), :] = hot(row == pick_s(col))

    def transposed(dst, src):
        for t in range(4):
            dst[:, t * 128:(t + 1) * 128] = jnp.transpose(src[t * 128:(t + 1) * 128, :].astype(F32)).astype(BF16)

    def column(row8):
        return jnp.transpose(jnp.broadcast_to(row8[0:1, :], (128, 128)))

    def matmul(dst, a, b):
        @pl.loop(0, 2)
        def _(t):
            dst[rows(t, 256), :] = dot(a[rows(t, 256), :], b()).astype(dst.dtype)

    def matmul8(dst, a, b):
        @pl.loop(0, 2)
        def _(t):
            dst[pl.ds(t * 4, 4)] = dot(a[rows(t, 256), :], b()).astype(BF16).reshape(4, 64, 512)

    def scatter8(kind, src, dst):
        for j in g_peers:
            send(kind, src.at[j], dst.at[g], dev_g(j))
        dst[g] = src[g]

    def flat(ref):
        return lambda: ref[...].reshape(512, 512)

    def whole(ref):
        return lambda: ref[...]

    arrived("left", lg)

    @pl.loop(0, 4)
    def _(t):
        for i in range(2):
            pick = hot((row0 == 64 * i + (col & 63)) & ((col >> 6) == 2 * t + i))
            tmp[pl.ds(pl.multiple_of(t * 128 + i * 64, 64), 64), :] = dot(lg[t], pick).astype(BF16)

    matmul(l_m, q_m, whole(tmp))
    transposed(l_t, l_m)

    arrived("weight", wfull.at[pl.ds(0, 7)])
    for n in range(8):
        for j in range(4):
            i = 16 * (8 * (n // 2) + 2 * j + n % 2)
            wnat[i:i + 16, :] = wfull[n, j]

    arrived("gain", gn)
    gain_k = gn[0]
    arrived("act", xc)
    arrived("stat", stg)

    @pl.loop(0, 4)
    def _(t):
        inv = column(stg[t, 0:8, :])
        normed = xc[t].astype(F32) * inv[:, 0:1]
        ni_c[rows(t), :] = (normed * gain_k).astype(BF16)

    matmul(p_c, ni_c, whole(wnat))
    matmul8(fc, l_m, whole(p_c))
    scatter8("fc", fc, fcr)
    arrived("right", rg)

    @pl.loop(0, 4)
    def _(t):
        for i in range(2):
            pick = hot((row0 == 64 * i + (pick_s(col) & 63)) & ((col & 7) == 2 * t + i))
            tmp[pl.ds(pl.multiple_of(t * 128 + i * 64, 64), 64), :] = dot(rg[t], pick).astype(BF16)

    @pl.loop(0, 4)
    def _(t):
        r_m[rows(t), :] = dot(hot(col == pick_s(row0 + t * 128)), tmp[...]).astype(BF16)

    transposed(r_t, r_m)

    arrived("fc", fcr.at[pl.ds(0, 7)])
    matmul8(mc, r_m, flat(fcr))
    scatter8("mc", mc, mcr)

    arrived("sto", xs)

    @pl.loop(0, 4)
    def _(t):
        inv = column(stg[t, 8:16, :])
        inv_s[t] = inv
        normed = xs[t].astype(F32) * inv[:, 0:1]
        ni_s[rows(t), :] = (normed * gain_k).astype(BF16)

    matmul(p_s, ni_s, whole(wnat))
    matmul8(fs, l_m, whole(p_s))
    scatter8("fs", fs, fsr)
    transposed(ni_t, ni_s)

    arrived("mc", mcr.at[pl.ds(0, 7)])

    @pl.loop(0, 4)
    def _(t):
        mixed = dot(q_t[rows(t), :], mcr[...].reshape(512, 512))
        outb[t] = (xc[t].astype(F32) + p_c[rows(t), :].astype(F32) * mixed).astype(BF16)

    arrived("grad", xg)

    @pl.loop(0, 4)
    def _(t):
        tmp[rows(t), :] = (xg[t].astype(F32) * p_s[rows(t), :].astype(F32)).astype(BF16)

    matmul8(am, q_m, whole(tmp))
    scatter8("am", am, amr)
    send_out("out", outb, handed, ring(job + 1))

    arrived("fs", fsr.at[pl.ds(0, 7)])
    matmul8(ms, r_m, flat(fsr))
    scatter8("ms", ms, msr)
    matmul(tmp2, s_t, flat(fsr))

    arrived("am", amr.at[pl.ds(0, 7)])
    matmul8(af, r_t, flat(amr))
    scatter8("af", af, afr)

    def pair_grads(dst, a, b):
        @pl.loop(0, 4)
        def _(t):
            for i in range(2):
                part = pl.ds(pl.multiple_of(t * 128 + i * 64, 64), 64)
                dst[t, :, i * 64:(i + 1) * 64] = dot_t(a[part, :], b[part, :]).astype(BF16)

    matmul(tmp, s_t, flat(amr))
    pair_grads(grp, tmp, tmp2)
    for j in turn:
        send("gr", grp.at[j], gr_out.at[k], owner_in(job, j))

    arrived("ms", msr.at[pl.ds(0, 7)])
    arrived("af", afr.at[pl.ds(0, 7)])

    @pl.loop(0, 4)
    def _(t):
        mixed = dot(q_t[rows(t), :], msr[...].reshape(512, 512))
        through = dot(l_t[rows(t), :], afr[...].reshape(512, 512))
        adj = (xg[t].astype(F32) * mixed + through).astype(BF16)
        ap[rows(t), :] = adj
        part = jnp.sum(adj.astype(F32) * p_s[rows(t), :].astype(F32), axis=1, keepdims=True)
        msum[t] = jnp.transpose(jnp.broadcast_to(part, (128, 128)))[0:8]

    for j in k_peers:
        send("msum", msum, msumr.at[k], dev_k(j))
    msumr[k] = msum[...]

    ggs[...] = jnp.zeros((8, 512), F32)

    @pl.loop(0, 4)
    def _(t):
        adj_norm = dot_t(ap[rows(t), :], wnat[...])
        an[rows(t), :] = adj_norm
        normed = xs[t].astype(F32) * inv_s[t, :, 0:1]
        ggs[...] += jnp.sum((adj_norm * normed).reshape(16, 8, 512), axis=0)

    for j in g_peers:
        send("gg", ggs, ggr.at[g], dev_g(j))
    ggr[g] = ggs[...]

    matmul(tmp, q_t, flat(afr))
    pair_grads(glp, tmp, p_s)
    for j in turn:
        send("gl", glp.at[j], gl_out.at[k], owner_in(job, j))

    arrived("msum", msumr.at[pl.ds(0, 3)])

    @pl.loop(0, 4)
    def _(t):
        total = msumr[0, t] + msumr[1, t] + msumr[2, t] + msumr[3, t]
        mean = column(total)[:, 0:1] * (1.0 / 2048)
        inv = inv_s[t, :, 0:1]
        normed = xs[t].astype(F32) * inv
        scaled = an[rows(t), :] * gain_k
        gxb[t] = (xg[t].astype(F32) + inv * (scaled - normed * mean)).astype(BF16)

    send_out("gx", gxb, gradh, ring(job - 1))

    @pl.loop(0, 4)
    def _(t):
        gws[t] = dot(ni_t[rows(t), :], ap[...]).astype(BF16).reshape(4, 2, 16, 512)

    for j in g_peers:
        send("gw", gws.at[lax.div(j, 2), :, lax.rem(j, 2)], gwr.at[g], dev_g(j))
    gwr[g] = gws[lax.div(g, 2), :, lax.rem(g, 2)]

    arrived("gg", ggr.at[pl.ds(0, 7)])
    summed = ggr[0]
    for j in range(1, 8):
        summed = summed + ggr[j]
    ggx[...] = jnp.sum(summed, axis=0, keepdims=True)
    for j in turn:
        send("ggx", ggx, gg_out.at[k], owner_in(job, j))
    arrived("gw", gwr.at[pl.ds(0, 7)])
    for t in range(4):
        acc = gwr[0, t].astype(F32)
        for j in range(1, 8):
            acc = acc + gwr[j, t].astype(F32)
        gwx[t] = acc.astype(BF16)
    for j in turn:
        send("gwx", gwx.at[j], gw_out.at[k], owner_in(job, j))

    arrived("gr", gr_out)
    arrived("gl", gl_out)
    arrived("ggx", gg_out)
    arrived("gwx", gw_out)
    arrived("gx", gradh)
    arrived("out", handed)

    for kind, ref in (
        ("w", wk),
        ("gain", gn),
        ("sto", xs),
        ("left", lg),
        ("right", rg),
        ("stat", stg),
        ("grad", xg),
        ("act", xc),
        ("weight", wfull.at[pl.ds(0, 7)]),
        ("fs", fsr.at[pl.ds(0, 7)]),
        ("am", amr.at[pl.ds(0, 7)]),
        ("fc", fcr.at[pl.ds(0, 7)]),
        ("ms", msr.at[pl.ds(0, 7)]),
        ("af", afr.at[pl.ds(0, 7)]),
        ("mc", mcr.at[pl.ds(0, 7)]),
        ("gw", gwr.at[pl.ds(0, 7)]),
        ("gg", ggr.at[pl.ds(0, 7)]),
        ("gr", grp),
        ("gl", glp),
        ("msum", msumr.at[pl.ds(0, 3)]),
        ("gwx", gwx),
        ("ggx", gg_out),
    ):
        wait(send_sem, kind, ref)
    sent_out("out", outb, ring(job + 1))
    sent_out("gx", gxb, ring(job - 1))


def finish_kernel(handed, gradh, gw, gg, gl, gr, handed_o, gradh_o, gw_o, gg_o, gl_o, gr_o):
    handed_o[...] = handed[...]
    gradh_o[...] = gradh[...]
    for j in range(4):
        gw_o[:, j, :] = gw[j].astype(F32)
        gg_o[0:1, j * 512:(j + 1) * 512] = gg[j]
    for src, dst in ((gl, gl_o), (gr, gr_o)):
        total = src[0].astype(F32) + src[1].astype(F32) + src[2].astype(F32) + src[3].astype(F32)
        dst[0] = total[:, 0:64]
        dst[1] = total[:, 64:128]


def section(n_pipe, act, sto, grd, gain, w, left, right):
    vmem = pl.BlockSpec(memory_space=pltpu.VMEM)
    hbm = pl.BlockSpec(memory_space=pl.ANY)
    rows_all = pltpu.VMEM((128, 2048), BF16)
    big = pltpu.VMEM((512, 512), BF16)
    parts = pltpu.VMEM((8, 64, 512), BF16)
    tokens = pltpu.VMEM((4, 128, 512), BF16)
    pair = pltpu.VMEM((64, 128), BF16)
    pairs = pltpu.VMEM((4, 64, 128), BF16)
    scratch = (
        [rows_all] * 2
        + [pltpu.VMEM((4, 16, 512), BF16), pair, pair]
        + [tokens] * 3
        + [pairs] * 2
        + [pltpu.VMEM((4, 16, 512), BF16), pltpu.VMEM((8, 4, 16, 512), BF16), big, pltpu.VMEM((4, 1, 512), F32)]
        + [pltpu.VMEM((16, 128), F32), pltpu.VMEM((4, 16, 128), F32), pltpu.VMEM((4, 128, 128), F32)]
        + [big] * 14
        + [parts] * 12
        + [big, pltpu.VMEM((512, 512), F32)]
        + [pltpu.VMEM((4, 4, 2, 16, 512), BF16), pltpu.VMEM((8, 4, 16, 512), BF16), pltpu.VMEM((4, 16, 512), BF16)]
        + [pltpu.VMEM((8, 512), F32), pltpu.VMEM((8, 8, 512), F32), pltpu.VMEM((1, 512), F32)]
        + [pltpu.VMEM((4, 8, 128), F32), pltpu.VMEM((4, 4, 8, 128), F32)]
        + [pairs] * 2
        + [tokens] * 2
        + [pltpu.SemaphoreType.DMA((len(KINDS),)), pltpu.SemaphoreType.DMA((len(KINDS),)), pltpu.SemaphoreType.DMA((2,))]
    )
    raw = pl.pallas_call(
        functools.partial(kernel, n_pipe),
        out_shape=(
            jax.ShapeDtypeStruct((128, 2048), BF16),
            jax.ShapeDtypeStruct((128, 2048), BF16),
            jax.ShapeDtypeStruct((4, 16, 512), BF16),
            jax.ShapeDtypeStruct((4, 1, 512), F32),
            jax.ShapeDtypeStruct((4, 64, 128), BF16),
            jax.ShapeDtypeStruct((4, 64, 128), BF16),
        ),
        in_specs=[hbm] * 3 + [vmem] * 4,
        out_specs=(hbm,) * 6,
        scratch_shapes=scratch,
        compiler_params=pltpu.CompilerParams(
            collective_id=0, has_side_effects=True, vmem_limit_bytes=58 * 1024 * 1024
        ),
    )(act, sto, grd, gain, w, left, right)
    return pl.pallas_call(
        finish_kernel,
        out_shape=(
            jax.ShapeDtypeStruct((128, 2048), BF16),
            jax.ShapeDtypeStruct((128, 2048), BF16),
            jax.ShapeDtypeStruct((16, 4, 512), F32),
            jax.ShapeDtypeStruct((1, 2048), F32),
            jax.ShapeDtypeStruct((2, 64, 64), F32),
            jax.ShapeDtypeStruct((2, 64, 64), F32),
        ),
        in_specs=[vmem] * 6,
        out_specs=(vmem,) * 6,
    )(*raw)


def shards(n_pipe, act_in, saved_in, grad_in, gain, weight, left_blocks, right_blocks):
    outs = section(n_pipe, act_in[0], saved_in[0], grad_in[0], gain, weight[0], left_blocks[0], right_blocks[0])
    handed, gradh, gw, gg, gl, gr = outs
    return (handed[None], gradh[None], gw[None], gg, gl[None], gr[None])


def solution(mesh):
    return jax.shard_map(
        functools.partial(shards, mesh.shape["pipe"]),
        mesh=mesh,
        in_specs=(
            P("pipe", "seq", None),
            P("pipe", "seq", None),
            P("pipe", "seq", None),
            P("pipe", None),
            P("pipe", "seq", None, None),
            P("pipe", "seq", None, None),
            P("pipe", "seq", None, None),
        ),
        out_specs=(
            P("pipe", "seq", None),
            P("pipe", "seq", None),
            P("pipe", "seq", None, None),
            P("pipe", None),
            P("pipe", "seq", None, None),
            P("pipe", "seq", None, None),
        ),
        check_vma=False,
    )
```

```python
import functools

import jax
import jax.numpy as jnp
from jax import lax
from jax.experimental import pallas as pl
from jax.experimental.pallas import tpu as pltpu
from jax.sharding import PartitionSpec as P

MESH = pl.DeviceIdType.MESH
F32 = jnp.float32
BF16 = jnp.bfloat16

KINDS = (
    "w", "gain", "sto", "left", "right", "stat", "grad", "act", "weight", "fs", "am", "fc", "ms", "af", "mc",
    "gw", "gg", "gr", "gl", "msum", "gwx", "ggx", "out", "gx",
)
SEM = {name: i for i, name in enumerate(KINDS)}


def dot(a, b):
    return lax.dot_general(a, b, (((1,), (0,)), ((), ())), preferred_element_type=F32)


def dot_t(a, b):
    return lax.dot_general(a, b, (((1,), (1,)), ((), ())), preferred_element_type=F32)


def kernel(
    n_pipe,
    act, sto, grd, gain, w, left, right,
    handed, gradh, gw_out, gg_out, gl_out, gr_out,
    act_v, sto_v, w_v, left_v, right_v, w4, lpk, rpk,
    xs, xg, xc, lg, rg, wk, wfull, wnat, gn, st, stg, inv_s,
    ni_s, ni_c, ni_t, tmp, tmp2, s_t, r_m, r_t, p_s, p_c,
    q_m, q_t, l_m, l_t,
    fs, am, fc, fsr, amr, fcr, ms, af, mc, msr, afr, mcr,
    ap, an, gm, gws, gwr, gwx, ggs, ggr, ggx, msum, msumr, glp, grp, outb, gxb,
    send_sem, recv_sem, token_sem, load_sem,
):
    loads = [
        pltpu.make_async_copy(src, dst, load_sem.at[i])
        for i, (src, dst) in enumerate(((w, w_v), (left, left_v), (right, right_v), (act, act_v), (sto, sto_v)))
    ]
    for load in loads:
        load.start()

    pipe = lax.axis_index("pipe")
    seq = lax.axis_index("seq")
    core = lax.rem(pipe, 2)
    chip = pipe - core
    x = lax.div(seq, 8)
    z = lax.rem(seq, 8)
    side = lax.rem(z, 2)
    k = lax.div(z, 2)
    half = 1 - core
    g = 2 * x + half
    job = chip + side

    def ring(p):
        return lax.rem(p + n_pipe, n_pipe)

    turn = [lax.rem(k + d, 4) for d in (2, 1, 3, 0)]
    order = [lax.rem(k + d, 4) for d in (2, 3, 1, 0)]

    def worker_of(section, j):
        odd = lax.rem(section, 2)
        return (section - odd + 1 - side, 8 * x + 2 * j + odd)

    def owner_in(section, j):
        return (section, 8 * x + 2 * j + half)

    k_peers = [lax.rem(k + d, 4) for d in (2, 1, 3)]
    g_peers = [lax.rem(g + d, 8) for d in (4, 5, 3, 6, 2, 7, 1)]

    def dev_k(j):
        return (pipe, 8 * x + 2 * j + side)

    def dev_g(j):
        return (chip + 1 - lax.rem(j, 2), 8 * lax.div(j, 2) + z)

    def send(kind, src, dst, dev, arrival=None):
        pltpu.make_async_remote_copy(
            src_ref=src, dst_ref=dst, send_sem=send_sem.at[SEM[kind]],
            recv_sem=recv_sem.at[SEM[kind]] if arrival is None else arrival,
            device_id=dev, device_id_type=MESH,
        ).start()

    def wait(sem, kind, ref):
        pltpu.make_async_copy(ref, ref, sem.at[SEM[kind]]).wait()

    def arrived(kind, ref):
        wait(recv_sem, kind, ref)

    def piece(which, j, ref):
        pltpu.make_async_copy(ref.at[j], ref.at[j], token_sem.at[which, j]).wait()

    met = [dev_k(j) for j in k_peers] + [dev_g(j) for j in g_peers]
    for d in (-1, 0, 1):
        met += [owner_in(ring(job + d), j) for j in range(4)]
        met += [worker_of(ring(pipe + d), j) for j in range(4)]
    barrier = pltpu.get_barrier_semaphore()
    for dev in met:
        pl.semaphore_signal(barrier, inc=1, device_id=dev, device_id_type=MESH)
    for load in loads[:3]:
        load.wait()
    for j in range(4):
        w4[j] = w_v[:, j, :]
    for src, dst in ((left_v, lpk), (right_v, rpk)):
        dst[:, 0:64] = src[0]
        dst[:, 64:128] = src[1]
    pl.semaphore_wait(barrier, len(met))

    def cols(j):
        if isinstance(j, int):
            return pl.ds(j * 512, 512)
        return pl.ds(pl.multiple_of(j * 512, 512), 512)

    def send_out(kind, src, dst, to, n):
        if n < 3:
            send(kind, src.at[turn[n]], dst.at[:, cols(k)], owner_in(to, turn[n]))
            return

        @pl.when(to == pipe)
        def _():
            pltpu.make_async_copy(src.at[k], dst.at[:, cols(k)], recv_sem.at[SEM[kind]]).start()

        @pl.when(to != pipe)
        def _():
            send(kind, src.at[k], dst.at[:, cols(k)], owner_in(to, k))

    def sent_out(kind, src, to):
        @pl.when(to == pipe)
        def _():
            wait(send_sem, kind, src.at[pl.ds(0, 3)])

        @pl.when(to != pipe)
        def _():
            wait(send_sem, kind, src)

    for j in turn:
        send("w", w4.at[j], wk.at[k], worker_of(pipe, j))
    for j in turn:
        send("left", lpk, lg.at[k], worker_of(pipe, j))
        send("gain", gain.at[:, cols(j)], gn.at[k], worker_of(pipe, j))

    def inv_row(x_ref):
        v = x_ref[...].astype(F32)
        inv = lax.rsqrt(jnp.sum(v * v, axis=1, keepdims=True) * (1.0 / 2048) + 1e-06)
        return jnp.transpose(jnp.broadcast_to(inv, (128, 128)))[0:8]

    loads[3].wait()
    st[0:8, :] = inv_row(act_v)
    loads[4].wait()
    st[8:16, :] = inv_row(sto_v)
    for j in turn:
        send("stat", st, stg.at[k], worker_of(pipe, j))
    for j in turn:
        send("act", act.at[:, cols(j)], xc.at[k], worker_of(pipe, j), token_sem.at[0, k])

    def nat(n, l):
        return 16 * (n >> 1) + 4 * (l >> 1) + 2 * (n & 1) + (l & 1)

    def pick_q(r):
        return 64 * ((r >> 3) & 1) + nat(r >> 4, r & 7)

    def pick_s(r):
        return 64 * (r & 7) + nat(r >> 6, (r >> 3) & 7)

    def hot(cond):
        return jnp.where(cond, 1.0, 0.0).astype(BF16)

    def rows(t, n=128):
        return pl.ds(pl.multiple_of(t * n, n), n)

    col = lax.broadcasted_iota(jnp.int32, (128, 512), 1)
    row0 = lax.broadcasted_iota(jnp.int32, (128, 512), 0)
    lane = lax.broadcasted_iota(jnp.int32, (128, 128), 1)
    line = lax.broadcasted_iota(jnp.int32, (128, 128), 0)

    arrived("w", wk)
    for j in g_peers:
        send("weight", wk, wfull.at[g], dev_g(j))
    wfull[g] = wk[...]

    q_m[...] = hot(lane == pick_q(line))
    q_t[...] = hot(line == pick_q(lane))

    @pl.loop(0, 4)
    def _(t):
        s_t[rows(t), :] = hot(row0 + t * 128 == pick_s(col))

    def column(row8):
        return jnp.transpose(jnp.broadcast_to(row8[0:1, :], (128, 128)))

    def matmul(dst, a, b):
        @pl.loop(0, 2)
        def _(t):
            dst[rows(t, 256), :] = dot(a[rows(t, 256), :], b()).astype(dst.dtype)

    def matmul8(dst, a, b):
        @pl.loop(0, 2)
        def _(t):
            dst[pl.ds(t * 4, 4)] = dot(a[rows(t, 256), :], b()).astype(BF16).reshape(4, 64, 512)

    def scatter8(kind, src, dst):
        for j in g_peers:
            send(kind, src.at[j], dst.at[g], dev_g(j))
        dst[g] = src[g]

    def slot(t):
        return pl.ds(pl.multiple_of(t * 16, 16), 16)

    def scatter_slot(kind, src, dst, t, value):
        src[:, slot(t), :] = value.astype(BF16).reshape(8, 16, 512)
        for j in g_peers:
            send(kind, src.at[j, slot(t)], dst.at[g, slot(t)], dev_g(j))
        dst[g, slot(t), :] = src[g, slot(t), :]

    def slot_rows(ref, t):
        return ref[:, slot(t), :].reshape(128, 512)

    def flat(ref):
        return lambda: ref[...].reshape(512, 512)

    arrived("left", lg)

    @pl.loop(0, 4)
    def _(t):
        pair = lg[t].astype(F32)
        both = jnp.where((line >> 6) == (lane >> 6), jnp.concatenate([pair, pair], axis=0), 0.0)
        mixer = dot(q_m[...], both.astype(BF16))
        l_m[t] = mixer.astype(BF16)
        l_t[t] = jnp.transpose(mixer).astype(BF16)

    for j in turn:
        send("right", rpk, rg.at[k], worker_of(pipe, j))
    for j in turn:
        send("sto", sto.at[:, cols(j)], xs.at[k], worker_of(pipe, j), token_sem.at[1, k])
    arrived("weight", wfull.at[pl.ds(0, 7)])
    for n in range(8):
        for j in range(4):
            i = 16 * (8 * (n // 2) + 2 * j + n % 2)
            wnat[i:i + 16, :] = wfull[n, j]

    arrived("gain", gn)
    gain_k = gn[0]
    arrived("stat", stg)
    for t in order:
        piece(0, t, xc)
        inv = column(stg[t, 0:8, :])
        normed = xc[t].astype(F32) * inv[:, 0:1]
        ni_c[rows(t), :] = (normed * gain_k).astype(BF16)
        p_c[rows(t), :] = dot(ni_c[rows(t), :], wnat[...]).astype(BF16)
        scatter_slot("fc", fc, fcr, t, dot(l_m[t], p_c[rows(t), :]))

    for j in turn:
        send("grad", grd.at[:, cols(j)], xg.at[k], worker_of(pipe, j), token_sem.at[2, k])

    arrived("right", rg)

    @pl.loop(0, 4)
    def _(t):
        for i in range(2):
            pick = hot((row0 == 64 * i + (pick_s(col) & 63)) & ((col & 7) == 2 * t + i))
            tmp[pl.ds(pl.multiple_of(t * 128 + i * 64, 64), 64), :] = dot(rg[t], pick).astype(BF16)

    @pl.loop(0, 4)
    def _(t):
        r_m[rows(t), :] = dot(hot(col == pick_s(row0 + t * 128)), tmp[...]).astype(BF16)

    def transposed(dst, src):
        for t in range(4):
            dst[:, t * 128:(t + 1) * 128] = jnp.transpose(src[t * 128:(t + 1) * 128, :].astype(F32)).astype(BF16)

    arrived("fc", fcr.at[pl.ds(0, 7)])
    matmul8(mc, r_m, flat(fcr))
    scatter8("mc", mc, mcr)
    transposed(r_t, r_m)

    for t in order:
        piece(1, t, xs)
        inv = column(stg[t, 8:16, :])
        inv_s[t] = inv
        normed = xs[t].astype(F32) * inv[:, 0:1]
        ni_s[rows(t), :] = (normed * gain_k).astype(BF16)
        p_s[rows(t), :] = dot(ni_s[rows(t), :], wnat[...]).astype(BF16)
        scatter_slot("fs", fs, fsr, t, dot(l_m[t], p_s[rows(t), :]))
    transposed(ni_t, ni_s)

    for t in order:
        piece(2, t, xg)
        adj = (xg[t].astype(F32) * p_s[rows(t), :].astype(F32)).astype(BF16)
        scatter_slot("am", am, amr, t, dot(q_m[...], adj))

    arrived("mc", mcr.at[pl.ds(0, 7)])

    @pl.loop(0, 4)
    def _(t):
        mixed = dot(q_t[...], slot_rows(mcr, t))
        outb[t] = (xc[t].astype(F32) + p_c[rows(t), :].astype(F32) * mixed).astype(BF16)

    for n in range(4):
        send_out("out", outb, handed, ring(job + 1), n)

    arrived("fs", fsr.at[pl.ds(0, 7)])
    matmul8(ms, r_m, flat(fsr))
    scatter8("ms", ms, msr)
    arrived("am", amr.at[pl.ds(0, 7)])
    matmul8(af, r_t, flat(amr))
    scatter8("af", af, afr)

    matmul(tmp2, s_t, flat(fsr))
    matmul(tmp, s_t, flat(amr))

    @pl.loop(0, 4)
    def _(t):
        for i in range(2):
            part = pl.ds(pl.multiple_of(t * 128 + i * 64, 64), 64)
            grp[t, :, i * 64:(i + 1) * 64] = dot_t(tmp[part, :], tmp2[part, :]).astype(BF16)

    for j in turn:
        send("gr", grp.at[j], gr_out.at[k], owner_in(job, j))

    arrived("ms", msr.at[pl.ds(0, 7)])

    @pl.loop(0, 4)
    def _(t):
        gm[rows(t), :] = xg[t].astype(F32) * dot(q_t[...], slot_rows(msr, t))

    arrived("af", afr.at[pl.ds(0, 7)])

    @pl.loop(0, 4)
    def _(t):
        adj = (gm[rows(t), :] + dot(l_t[t], slot_rows(afr, t))).astype(BF16)
        ap[rows(t), :] = adj
        part = jnp.sum(adj.astype(F32) * p_s[rows(t), :].astype(F32), axis=1, keepdims=True)
        msum[t] = jnp.transpose(jnp.broadcast_to(part, (128, 128)))[0:8]

    for j in k_peers:
        send("msum", msum, msumr.at[k], dev_k(j))
    msumr[k] = msum[...]

    ggs[...] = jnp.zeros((8, 512), F32)

    @pl.loop(0, 4)
    def _(t):
        adj_norm = dot_t(ap[rows(t), :], wnat[...])
        inv = inv_s[t, :, 0:1]
        normed = xs[t].astype(F32) * inv
        an[rows(t), :] = xg[t].astype(F32) + inv * (adj_norm * gain_k)
        ggs[...] += jnp.sum((adj_norm * normed).reshape(16, 8, 512), axis=0)

    for j in g_peers:
        send("gg", ggs, ggr.at[g], dev_g(j))
    ggr[g] = ggs[...]

    @pl.loop(0, 4)
    def _(t):
        gws[t] = dot(ni_t[rows(t), :], ap[...]).astype(BF16).reshape(4, 2, 16, 512)

    for j in g_peers:
        send("gw", gws.at[lax.div(j, 2), :, lax.rem(j, 2)], gwr.at[g], dev_g(j))
    gwr[g] = gws[lax.div(g, 2), :, lax.rem(g, 2)]

    @pl.loop(0, 4)
    def _(t):
        tmp[rows(t), :] = dot(q_t[...], slot_rows(afr, t)).astype(BF16)
        for i in range(2):
            part = pl.ds(pl.multiple_of(t * 128 + i * 64, 64), 64)
            glp[t, :, i * 64:(i + 1) * 64] = dot_t(tmp[part, :], p_s[part, :]).astype(BF16)

    for j in turn:
        send("gl", glp.at[j], gl_out.at[k], owner_in(job, j))

    arrived("msum", msumr.at[pl.ds(0, 3)])

    for n, t in enumerate(turn):
        total = msumr[0, t] + msumr[1, t] + msumr[2, t] + msumr[3, t]
        inv = inv_s[t]
        weight = (inv * inv * column(total))[:, 0:1] * (1.0 / 2048)
        gxb[t] = (an[rows(t), :] - xs[t].astype(F32) * weight).astype(BF16)
        send_out("gx", gxb, gradh, ring(job - 1), n)

    arrived("gg", ggr.at[pl.ds(0, 7)])
    summed = ggr[0]
    for j in range(1, 8):
        summed = summed + ggr[j]
    ggx[...] = jnp.sum(summed, axis=0, keepdims=True)
    for j in turn:
        send("ggx", ggx, gg_out.at[k], owner_in(job, j))
    arrived("gw", gwr.at[pl.ds(0, 7)])
    for t in range(4):
        acc = gwr[0, t].astype(F32)
        for j in range(1, 8):
            acc = acc + gwr[j, t].astype(F32)
        gwx[t] = acc.astype(BF16)
    for j in turn:
        send("gwx", gwx.at[j], gw_out.at[k], owner_in(job, j))

    arrived("gr", gr_out)
    arrived("gl", gl_out)
    arrived("ggx", gg_out)
    arrived("gwx", gw_out)
    arrived("gx", gradh)
    arrived("out", handed)

    for kind, ref in (
        ("w", wk),
        ("gain", gn),
        ("sto", xs),
        ("left", lg),
        ("right", rg),
        ("stat", stg),
        ("grad", xg),
        ("act", xc),
        ("weight", wfull.at[pl.ds(0, 7)]),
        ("fs", fsr.at[pl.ds(0, 7)]),
        ("am", amr.at[pl.ds(0, 7)]),
        ("fc", fcr.at[pl.ds(0, 7)]),
        ("ms", msr.at[pl.ds(0, 7)]),
        ("af", afr.at[pl.ds(0, 7)]),
        ("mc", mcr.at[pl.ds(0, 7)]),
        ("gw", gwr.at[pl.ds(0, 7)]),
        ("gg", ggr.at[pl.ds(0, 7)]),
        ("gr", grp),
        ("gl", glp),
        ("msum", msumr.at[pl.ds(0, 3)]),
        ("gwx", gwx),
        ("ggx", gg_out),
    ):
        wait(send_sem, kind, ref)
    sent_out("out", outb, ring(job + 1))
    sent_out("gx", gxb, ring(job - 1))


def finish_kernel(handed, gradh, gw, gg, gl, gr, handed_o, gradh_o, gw_o, gg_o, gl_o, gr_o):
    handed_o[...] = handed[...]
    gradh_o[...] = gradh[...]
    for j in range(4):
        gw_o[:, j, :] = gw[j].astype(F32)
        gg_o[0:1, j * 512:(j + 1) * 512] = gg[j]
    for src, dst in ((gl, gl_o), (gr, gr_o)):
        total = src[0].astype(F32) + src[1].astype(F32) + src[2].astype(F32) + src[3].astype(F32)
        dst[0] = total[:, 0:64]
        dst[1] = total[:, 64:128]


def section(n_pipe, act, sto, grd, gain, w, left, right):
    vmem = pl.BlockSpec(memory_space=pltpu.VMEM)
    hbm = pl.BlockSpec(memory_space=pl.ANY)
    rows_all = pltpu.VMEM((128, 2048), BF16)
    big = pltpu.VMEM((512, 512), BF16)
    parts = pltpu.VMEM((8, 64, 512), BF16)
    tokens = pltpu.VMEM((4, 128, 512), BF16)
    pair = pltpu.VMEM((64, 128), BF16)
    pairs = pltpu.VMEM((4, 64, 128), BF16)
    square = pltpu.VMEM((128, 128), BF16)
    squares = pltpu.VMEM((4, 128, 128), BF16)
    scratch = (
        [rows_all] * 2
        + [pltpu.VMEM((16, 4, 512), BF16), pltpu.VMEM((2, 64, 64), BF16), pltpu.VMEM((2, 64, 64), BF16)]
        + [pltpu.VMEM((4, 16, 512), BF16), pair, pair]
        + [tokens] * 3
        + [pairs] * 2
        + [pltpu.VMEM((4, 16, 512), BF16), pltpu.VMEM((8, 4, 16, 512), BF16), big, pltpu.VMEM((4, 1, 512), F32)]
        + [pltpu.VMEM((16, 128), F32), pltpu.VMEM((4, 16, 128), F32), pltpu.VMEM((4, 128, 128), F32)]
        + [big] * 10
        + [square, square, squares, squares]
        + [parts] * 12
        + [big, pltpu.VMEM((512, 512), F32), pltpu.VMEM((512, 512), F32)]
        + [pltpu.VMEM((4, 4, 2, 16, 512), BF16), pltpu.VMEM((8, 4, 16, 512), BF16), pltpu.VMEM((4, 16, 512), BF16)]
        + [pltpu.VMEM((8, 512), F32), pltpu.VMEM((8, 8, 512), F32), pltpu.VMEM((1, 512), F32)]
        + [pltpu.VMEM((4, 8, 128), F32), pltpu.VMEM((4, 4, 8, 128), F32)]
        + [pairs] * 2
        + [tokens] * 2
        + [pltpu.SemaphoreType.DMA((len(KINDS),)), pltpu.SemaphoreType.DMA((len(KINDS),))]
        + [pltpu.SemaphoreType.DMA((3, 4)), pltpu.SemaphoreType.DMA((5,))]
    )
    raw = pl.pallas_call(
        functools.partial(kernel, n_pipe),
        out_shape=(
            jax.ShapeDtypeStruct((128, 2048), BF16),
            jax.ShapeDtypeStruct((128, 2048), BF16),
            jax.ShapeDtypeStruct((4, 16, 512), BF16),
            jax.ShapeDtypeStruct((4, 1, 512), F32),
            jax.ShapeDtypeStruct((4, 64, 128), BF16),
            jax.ShapeDtypeStruct((4, 64, 128), BF16),
        ),
        in_specs=[hbm] * 7,
        out_specs=(hbm,) * 6,
        scratch_shapes=scratch,
        compiler_params=pltpu.CompilerParams(
            collective_id=0, has_side_effects=True, vmem_limit_bytes=58 * 1024 * 1024
        ),
    )(act, sto, grd, gain, w, left, right)
    return pl.pallas_call(
        finish_kernel,
        out_shape=(
            jax.ShapeDtypeStruct((128, 2048), BF16),
            jax.ShapeDtypeStruct((128, 2048), BF16),
            jax.ShapeDtypeStruct((16, 4, 512), F32),
            jax.ShapeDtypeStruct((1, 2048), F32),
            jax.ShapeDtypeStruct((2, 64, 64), F32),
            jax.ShapeDtypeStruct((2, 64, 64), F32),
        ),
        in_specs=[vmem] * 6,
        out_specs=(vmem,) * 6,
    )(*raw)


def shards(n_pipe, act_in, saved_in, grad_in, gain, weight, left_blocks, right_blocks):
    outs = section(n_pipe, act_in[0], saved_in[0], grad_in[0], gain, weight[0], left_blocks[0], right_blocks[0])
    handed, gradh, gw, gg, gl, gr = outs
    return (handed[None], gradh[None], gw[None], gg, gl[None], gr[None])


def solution(mesh):
    return jax.shard_map(
        functools.partial(shards, mesh.shape["pipe"]),
        mesh=mesh,
        in_specs=(
            P("pipe", "seq", None),
            P("pipe", "seq", None),
            P("pipe", "seq", None),
            P("pipe", None),
            P("pipe", "seq", None, None),
            P("pipe", "seq", None, None),
            P("pipe", "seq", None, None),
        ),
        out_specs=(
            P("pipe", "seq", None),
            P("pipe", "seq", None),
            P("pipe", "seq", None, None),
            P("pipe", None),
            P("pipe", "seq", None, None),
            P("pipe", "seq", None, None),
        ),
        check_vma=False,
    )
```

```python
import functools

import jax
import jax.numpy as jnp
from jax import lax
from jax.experimental import pallas as pl
from jax.experimental.pallas import tpu as pltpu
from jax.sharding import PartitionSpec as P

MESH = pl.DeviceIdType.MESH
F32 = jnp.float32
BF16 = jnp.bfloat16

KINDS = (
    "w", "gain", "sto", "left", "right", "stat", "grad", "act", "weight", "fs", "am", "fc", "ms", "af", "af2", "mc",
    "gw", "gg", "gr", "gl", "msum", "msum2", "gwx", "ggx", "out", "gx",
)
SEM = {name: i for i, name in enumerate(KINDS)}


HALVES = (("af", (0, 2)), ("af2", (1, 3)))


def dot(a, b):
    return lax.dot_general(a, b, (((1,), (0,)), ((), ())), preferred_element_type=F32)


def dot_t(a, b):
    return lax.dot_general(a, b, (((1,), (1,)), ((), ())), preferred_element_type=F32)


def kernel(
    n_pipe,
    act, sto, grd, gain, w, left, right,
    handed, gradh, gw_out, gg_out, gl_out, gr_out,
    act_v, sto_v, w_v, left_v, right_v, w4, lpk, rpk,
    xs, xg, xc, lg, rg, wk, wfull, wnat, gn, st, stg, inv_s,
    ni_s, ni_c, ni_t, tmp, tmp2, s_t, r_m, r_t, p_s, p_c,
    q_m, q_t, l_m, l_t,
    fs, am, fc, fsr, amr, fcr, ms, af, mc, msr, afr, mcr,
    ap, an, gm, gws, gwr, gwx, ggs, ggw, ggr, ggx, msum, msumr, glp, grp, outb, gxb,
    send_sem, recv_sem, token_sem, load_sem,
):
    loads = [
        pltpu.make_async_copy(src, dst, load_sem.at[i])
        for i, (src, dst) in enumerate(((w, w_v), (left, left_v), (right, right_v), (act, act_v), (sto, sto_v)))
    ]
    for load in loads:
        load.start()

    pipe = lax.axis_index("pipe")
    seq = lax.axis_index("seq")
    core = lax.rem(pipe, 2)
    chip = pipe - core
    x = lax.div(seq, 8)
    z = lax.rem(seq, 8)
    side = lax.rem(z, 2)
    k = lax.div(z, 2)
    half = 1 - core
    g = 2 * x + half
    job = chip + side

    def ring(p):
        return lax.rem(p + n_pipe, n_pipe)

    turn = [lax.rem(k + d, 4) for d in (2, 1, 3, 0)]
    order = [lax.rem(k + d, 4) for d in (2, 3, 1, 0)]

    def worker_of(section, j):
        odd = lax.rem(section, 2)
        return (section - odd + 1 - side, 8 * x + 2 * j + odd)

    def owner_in(section, j):
        return (section, 8 * x + 2 * j + half)

    k_peers = [lax.rem(k + d, 4) for d in (2, 1, 3)]
    g_peers = [lax.rem(g + d, 8) for d in (4, 5, 3, 6, 2, 7, 1)]

    def dev_k(j):
        return (pipe, 8 * x + 2 * j + side)

    def dev_g(j):
        return (chip + 1 - lax.rem(j, 2), 8 * lax.div(j, 2) + z)

    def send(kind, src, dst, dev, arrival=None):
        pltpu.make_async_remote_copy(
            src_ref=src, dst_ref=dst, send_sem=send_sem.at[SEM[kind]],
            recv_sem=recv_sem.at[SEM[kind]] if arrival is None else arrival,
            device_id=dev, device_id_type=MESH,
        ).start()

    def wait(sem, kind, ref):
        pltpu.make_async_copy(ref, ref, sem.at[SEM[kind]]).wait()

    def arrived(kind, ref):
        wait(recv_sem, kind, ref)

    def piece(which, j, ref):
        pltpu.make_async_copy(ref.at[j], ref.at[j], token_sem.at[which, j]).wait()

    met = [dev_k(j) for j in k_peers] + [dev_g(j) for j in g_peers]
    for d in (-1, 0, 1):
        met += [owner_in(ring(job + d), j) for j in range(4)]
        met += [worker_of(ring(pipe + d), j) for j in range(4)]
    barrier = pltpu.get_barrier_semaphore()
    for dev in met:
        pl.semaphore_signal(barrier, inc=1, device_id=dev, device_id_type=MESH)
    for load in loads[:3]:
        load.wait()
    for j in range(4):
        w4[j] = w_v[:, j, :]
    for src, dst in ((left_v, lpk), (right_v, rpk)):
        dst[:, 0:64] = src[0]
        dst[:, 64:128] = src[1]
    pl.semaphore_wait(barrier, len(met))

    def cols(j):
        if isinstance(j, int):
            return pl.ds(j * 512, 512)
        return pl.ds(pl.multiple_of(j * 512, 512), 512)

    def send_out(kind, src, dst, to, j):
        stays = jnp.logical_and(to == pipe, k == j)

        @pl.when(stays)
        def _():
            pltpu.make_async_copy(src.at[j], dst.at[:, cols(k)], recv_sem.at[SEM[kind]]).start()

        @pl.when(jnp.logical_not(stays))
        def _():
            send(kind, src.at[j], dst.at[:, cols(k)], owner_in(to, j))

    def sent_out(kind, src, to):
        @pl.when(to == pipe)
        def _():
            wait(send_sem, kind, src.at[pl.ds(0, 3)])

        @pl.when(to != pipe)
        def _():
            wait(send_sem, kind, src)

    for j in turn:
        send("w", w4.at[j], wk.at[k], worker_of(pipe, j))
    for j in turn:
        send("left", lpk, lg.at[k], worker_of(pipe, j))
        send("gain", gain.at[:, cols(j)], gn.at[k], worker_of(pipe, j))

    def inv_row(x_ref):
        v = x_ref[...].astype(F32)
        inv = lax.rsqrt(jnp.sum(v * v, axis=1, keepdims=True) * (1.0 / 2048) + 1e-06)
        return jnp.transpose(jnp.broadcast_to(inv, (128, 128)))[0:8]

    loads[3].wait()
    st[0:8, :] = inv_row(act_v)
    loads[4].wait()
    st[8:16, :] = inv_row(sto_v)
    for j in turn:
        send("stat", st, stg.at[k], worker_of(pipe, j))
    for j in turn:
        send("act", act.at[:, cols(j)], xc.at[k], worker_of(pipe, j), token_sem.at[0, k])

    def nat(n, l):
        return 16 * (n >> 1) + 4 * (l >> 1) + 2 * (n & 1) + (l & 1)

    def pick_q(r):
        return 64 * ((r >> 3) & 1) + nat(r >> 4, r & 7)

    def pick_s(r):
        return 64 * (r & 7) + nat(r >> 6, (r >> 3) & 7)

    def hot(cond):
        return jnp.where(cond, 1.0, 0.0).astype(BF16)

    def rows(t, n=128):
        if isinstance(t, int):
            return pl.ds(t * n, n)
        return pl.ds(pl.multiple_of(t * n, n), n)

    col = lax.broadcasted_iota(jnp.int32, (128, 512), 1)
    row0 = lax.broadcasted_iota(jnp.int32, (128, 512), 0)
    lane = lax.broadcasted_iota(jnp.int32, (128, 128), 1)
    line = lax.broadcasted_iota(jnp.int32, (128, 128), 0)

    arrived("w", wk)
    for j in g_peers:
        send("weight", wk, wfull.at[g], dev_g(j))
    wfull[g] = wk[...]

    q_m[...] = hot(lane == pick_q(line))
    q_t[...] = hot(line == pick_q(lane))

    @pl.loop(0, 4)
    def _(t):
        s_t[rows(t), :] = hot(row0 + t * 128 == pick_s(col))

    def column(row8):
        return jnp.transpose(jnp.broadcast_to(row8[0:1, :], (128, 128)))

    def matmul(dst, a, b):
        @pl.loop(0, 2)
        def _(t):
            dst[rows(t, 256), :] = dot(a[rows(t, 256), :], b()).astype(dst.dtype)

    def matmul8(dst, a, b):
        @pl.loop(0, 2)
        def _(t):
            dst[pl.ds(t * 4, 4)] = dot(a[rows(t, 256), :], b()).astype(BF16).reshape(4, 64, 512)

    def scatter8(kind, src, dst):
        for j in g_peers:
            send(kind, src.at[j], dst.at[g], dev_g(j))
        dst[g] = src[g]

    def slot(t):
        if isinstance(t, int):
            return pl.ds(t * 16, 16)
        return pl.ds(pl.multiple_of(t * 16, 16), 16)

    def scatter_slot(kind, src, dst, t, value):
        src[:, slot(t), :] = value.astype(BF16).reshape(8, 16, 512)
        for j in g_peers:
            send(kind, src.at[j, slot(t)], dst.at[g, slot(t)], dev_g(j))
        dst[g, slot(t), :] = src[g, slot(t), :]

    def slot_rows(ref, t):
        return ref[:, slot(t), :].reshape(128, 512)

    def flat(ref):
        return lambda: ref[...].reshape(512, 512)

    arrived("left", lg)

    @pl.loop(0, 4)
    def _(t):
        pair = lg[t].astype(F32)
        both = jnp.where((line >> 6) == (lane >> 6), jnp.concatenate([pair, pair], axis=0), 0.0)
        mixer = dot(q_m[...], both.astype(BF16))
        l_m[t] = mixer.astype(BF16)
        l_t[t] = jnp.transpose(mixer).astype(BF16)

    for j in turn:
        send("right", rpk, rg.at[k], worker_of(pipe, j))
    for j in turn:
        send("sto", sto.at[:, cols(j)], xs.at[k], worker_of(pipe, j), token_sem.at[1, k])
    arrived("weight", wfull.at[pl.ds(0, 7)])
    for n in range(8):
        for j in range(4):
            i = 16 * (8 * (n // 2) + 2 * j + n % 2)
            wnat[i:i + 16, :] = wfull[n, j]

    arrived("gain", gn)
    gain_k = gn[0]
    arrived("stat", stg)
    for t in order:
        piece(0, t, xc)
        inv = column(stg[t, 0:8, :])
        normed = xc[t].astype(F32) * inv[:, 0:1]
        ni_c[rows(t), :] = (normed * gain_k).astype(BF16)
        p_c[rows(t), :] = dot(ni_c[rows(t), :], wnat[...]).astype(BF16)
        scatter_slot("fc", fc, fcr, t, dot(l_m[t], p_c[rows(t), :]))

    for j in turn:
        send("grad", grd.at[:, cols(j)], xg.at[k], worker_of(pipe, j), token_sem.at[2, k])

    arrived("right", rg)

    @pl.loop(0, 4)
    def _(t):
        for i in range(2):
            pick = hot((row0 == 64 * i + (pick_s(col) & 63)) & ((col & 7) == 2 * t + i))
            tmp[pl.ds(pl.multiple_of(t * 128 + i * 64, 64), 64), :] = dot(rg[t], pick).astype(BF16)

    @pl.loop(0, 4)
    def _(t):
        r_m[rows(t), :] = dot(hot(col == pick_s(row0 + t * 128)), tmp[...]).astype(BF16)

    def transposed(dst, src):
        for t in range(4):
            dst[:, t * 128:(t + 1) * 128] = jnp.transpose(src[t * 128:(t + 1) * 128, :].astype(F32)).astype(BF16)

    arrived("fc", fcr.at[pl.ds(0, 7)])
    matmul8(mc, r_m, flat(fcr))
    scatter8("mc", mc, mcr)
    transposed(r_t, r_m)

    for t in order:
        piece(1, t, xs)
        inv = column(stg[t, 8:16, :])
        inv_s[t] = inv
        normed = xs[t].astype(F32) * inv[:, 0:1]
        ni_s[rows(t), :] = (normed * gain_k).astype(BF16)
        p_s[rows(t), :] = dot(ni_s[rows(t), :], wnat[...]).astype(BF16)
        scatter_slot("fs", fs, fsr, t, dot(l_m[t], p_s[rows(t), :]))
    transposed(ni_t, ni_s)

    for t in order:
        piece(2, t, xg)
        adj = (xg[t].astype(F32) * p_s[rows(t), :].astype(F32)).astype(BF16)
        scatter_slot("am", am, amr, t, dot(q_m[...], adj))

    arrived("mc", mcr.at[pl.ds(0, 7)])

    @pl.loop(0, 4)
    def _(t):
        mixed = dot(q_t[...], slot_rows(mcr, t))
        outb[t] = (xc[t].astype(F32) + p_c[rows(t), :].astype(F32) * mixed).astype(BF16)

    for j in (0, 2, 1, 3):
        send_out("out", outb, handed, ring(job + 1), j)

    arrived("fs", fsr.at[pl.ds(0, 7)])
    matmul8(ms, r_m, flat(fsr))
    scatter8("ms", ms, msr)
    arrived("am", amr.at[pl.ds(0, 7)])
    matmul8(af, r_t, flat(amr))
    for kind, pair in HALVES:
        for j in g_peers:
            for t in pair:
                send(kind, af.at[j, slot(t)], afr.at[g, slot(t)], dev_g(j))
    afr[g] = af[g]

    matmul(tmp2, s_t, flat(fsr))
    matmul(tmp, s_t, flat(amr))

    @pl.loop(0, 4)
    def _(t):
        for i in range(2):
            part = pl.ds(pl.multiple_of(t * 128 + i * 64, 64), 64)
            grp[t, :, i * 64:(i + 1) * 64] = dot_t(tmp[part, :], tmp2[part, :]).astype(BF16)

    for j in turn:
        send("gr", grp.at[j], gr_out.at[k], owner_in(job, j))

    arrived("ms", msr.at[pl.ds(0, 7)])

    @pl.loop(0, 4)
    def _(t):
        gm[rows(t), :] = xg[t].astype(F32) * dot(q_t[...], slot_rows(msr, t))

    ggs[...] = jnp.zeros((8, 512), F32)

    def adjoint_proj(h):
        kind, pair = HALVES[h]
        arrived(kind, afr.at[pl.ds(0, 7), pl.ds(0, 32)])
        sums = []
        for t in pair:
            adj = (gm[rows(t), :] + dot(l_t[t], slot_rows(afr, t))).astype(BF16)
            ap[rows(t), :] = adj
            part = jnp.sum(adj.astype(F32) * p_s[rows(t), :].astype(F32), axis=1, keepdims=True)
            sums.append(jnp.transpose(jnp.broadcast_to(part, (128, 128)))[0:4])
        msum[h] = jnp.concatenate(sums, axis=0)
        for j in k_peers:
            send("msum2" if h else "msum", msum.at[h], msumr.at[h, k], dev_k(j))
        msumr[h, k] = msum[h]

    def adjoint_norm(h):
        for t in HALVES[h][1]:
            adj_norm = dot_t(ap[rows(t), :], wnat[...])
            inv = inv_s[t, :, 0:1]
            normed = xs[t].astype(F32) * inv
            an[rows(t), :] = xg[t].astype(F32) + inv * (adj_norm * gain_k)
            ggs[...] += jnp.sum((adj_norm * normed).reshape(16, 8, 512), axis=0)

    def input_grad(h):
        arrived("msum2" if h else "msum", msumr.at[h, pl.ds(0, 3)])
        total = msumr[h, 0] + msumr[h, 1] + msumr[h, 2] + msumr[h, 3]
        for n, t in enumerate(HALVES[h][1]):
            inv = inv_s[t]
            weight = (inv * inv * column(total[4 * n:4 * n + 4]))[:, 0:1] * (1.0 / 2048)
            gxb[t] = (an[rows(t), :] - xs[t].astype(F32) * weight).astype(BF16)
            send_out("gx", gxb, gradh, ring(job - 1), t)

    adjoint_proj(0)
    adjoint_norm(0)
    adjoint_proj(1)

    @pl.loop(0, 4)
    def _(t):
        gws[t] = dot(ni_t[rows(t), :], ap[...]).astype(BF16).reshape(4, 2, 16, 512)

    for j in g_peers:
        send("gw", gws.at[lax.div(j, 2), :, lax.rem(j, 2)], gwr.at[g], dev_g(j))
    gwr[g] = gws[lax.div(g, 2), :, lax.rem(g, 2)]
    adjoint_norm(1)

    @pl.loop(0, 4)
    def _(t):
        tmp[rows(t), :] = dot(q_t[...], slot_rows(afr, t)).astype(BF16)
        for i in range(2):
            part = pl.ds(pl.multiple_of(t * 128 + i * 64, 64), 64)
            glp[t, :, i * 64:(i + 1) * 64] = dot_t(tmp[part, :], p_s[part, :]).astype(BF16)

    for j in turn:
        send("gl", glp.at[j], gl_out.at[k], owner_in(job, j))

    ggw[...] = jnp.sum(ggs[...], axis=0, keepdims=True)
    for j in g_peers:
        send("gg", ggw, ggr.at[g], dev_g(j))
    ggr[g] = ggw[...]
    input_grad(0)
    input_grad(1)

    arrived("gg", ggr.at[pl.ds(0, 7)])
    summed = ggr[0]
    for j in range(1, 8):
        summed = summed + ggr[j]
    ggx[...] = summed
    for j in turn:
        send("ggx", ggx, gg_out.at[k], owner_in(job, j))
    arrived("gw", gwr.at[pl.ds(0, 7)])
    for t in range(4):
        acc = gwr[0, t].astype(F32)
        for j in range(1, 8):
            acc = acc + gwr[j, t].astype(F32)
        gwx[t] = acc.astype(BF16)
    for j in turn:
        send("gwx", gwx.at[j], gw_out.at[k], owner_in(job, j))

    arrived("gr", gr_out)
    arrived("gl", gl_out)
    arrived("ggx", gg_out)
    arrived("gwx", gw_out)
    arrived("gx", gradh)
    arrived("out", handed)

    for kind, ref in (
        ("w", wk),
        ("gain", gn),
        ("sto", xs),
        ("left", lg),
        ("right", rg),
        ("stat", stg),
        ("grad", xg),
        ("act", xc),
        ("weight", wfull.at[pl.ds(0, 7)]),
        ("fs", fsr.at[pl.ds(0, 7)]),
        ("am", amr.at[pl.ds(0, 7)]),
        ("fc", fcr.at[pl.ds(0, 7)]),
        ("ms", msr.at[pl.ds(0, 7)]),
        ("af", afr.at[pl.ds(0, 7), pl.ds(0, 32)]),
        ("af2", afr.at[pl.ds(0, 7), pl.ds(0, 32)]),
        ("mc", mcr.at[pl.ds(0, 7)]),
        ("gw", gwr.at[pl.ds(0, 7)]),
        ("gg", ggr.at[pl.ds(0, 7)]),
        ("gr", grp),
        ("gl", glp),
        ("msum", msumr.at[0, pl.ds(0, 3)]),
        ("msum2", msumr.at[1, pl.ds(0, 3)]),
        ("gwx", gwx),
        ("ggx", gg_out),
    ):
        wait(send_sem, kind, ref)
    sent_out("out", outb, ring(job + 1))
    sent_out("gx", gxb, ring(job - 1))


def finish_kernel(handed, gradh, gw, gg, gl, gr, handed_o, gradh_o, gw_o, gg_o, gl_o, gr_o, sems):
    copies = [
        pltpu.make_async_copy(handed, handed_o, sems.at[0]),
        pltpu.make_async_copy(gradh, gradh_o, sems.at[1]),
    ]
    for copy in copies:
        copy.start()
    for j in range(4):
        gw_o[:, j, :] = gw[j].astype(F32)
        gg_o[0:1, j * 512:(j + 1) * 512] = gg[j]
    for src, dst in ((gl, gl_o), (gr, gr_o)):
        total = src[0].astype(F32) + src[1].astype(F32) + src[2].astype(F32) + src[3].astype(F32)
        dst[0] = total[:, 0:64]
        dst[1] = total[:, 64:128]
    for copy in copies:
        copy.wait()


def section(n_pipe, act, sto, grd, gain, w, left, right):
    vmem = pl.BlockSpec(memory_space=pltpu.VMEM)
    hbm = pl.BlockSpec(memory_space=pl.ANY)
    rows_all = pltpu.VMEM((128, 2048), BF16)
    big = pltpu.VMEM((512, 512), BF16)
    parts = pltpu.VMEM((8, 64, 512), BF16)
    tokens = pltpu.VMEM((4, 128, 512), BF16)
    pair = pltpu.VMEM((64, 128), BF16)
    pairs = pltpu.VMEM((4, 64, 128), BF16)
    square = pltpu.VMEM((128, 128), BF16)
    squares = pltpu.VMEM((4, 128, 128), BF16)
    scratch = (
        [rows_all] * 2
        + [pltpu.VMEM((16, 4, 512), BF16), pltpu.VMEM((2, 64, 64), BF16), pltpu.VMEM((2, 64, 64), BF16)]
        + [pltpu.VMEM((4, 16, 512), BF16), pair, pair]
        + [tokens] * 3
        + [pairs] * 2
        + [pltpu.VMEM((4, 16, 512), BF16), pltpu.VMEM((8, 4, 16, 512), BF16), big, pltpu.VMEM((4, 1, 512), F32)]
        + [pltpu.VMEM((16, 128), F32), pltpu.VMEM((4, 16, 128), F32), pltpu.VMEM((4, 128, 128), F32)]
        + [big] * 10
        + [square, square, squares, squares]
        + [parts] * 12
        + [big, pltpu.VMEM((512, 512), F32), pltpu.VMEM((512, 512), F32)]
        + [pltpu.VMEM((4, 4, 2, 16, 512), BF16), pltpu.VMEM((8, 4, 16, 512), BF16), pltpu.VMEM((4, 16, 512), BF16)]
        + [pltpu.VMEM((8, 512), F32), pltpu.VMEM((1, 512), F32), pltpu.VMEM((8, 1, 512), F32), pltpu.VMEM((1, 512), F32)]
        + [pltpu.VMEM((2, 8, 128), F32), pltpu.VMEM((2, 4, 8, 128), F32)]
        + [pairs] * 2
        + [tokens] * 2
        + [pltpu.SemaphoreType.DMA((len(KINDS),)), pltpu.SemaphoreType.DMA((len(KINDS),))]
        + [pltpu.SemaphoreType.DMA((3, 4)), pltpu.SemaphoreType.DMA((5,))]
    )
    raw = pl.pallas_call(
        functools.partial(kernel, n_pipe),
        out_shape=(
            jax.ShapeDtypeStruct((128, 2048), BF16),
            jax.ShapeDtypeStruct((128, 2048), BF16),
            jax.ShapeDtypeStruct((4, 16, 512), BF16),
            jax.ShapeDtypeStruct((4, 1, 512), F32),
            jax.ShapeDtypeStruct((4, 64, 128), BF16),
            jax.ShapeDtypeStruct((4, 64, 128), BF16),
        ),
        in_specs=[pl.BlockSpec(memory_space=pltpu.HBM)] * 7,
        out_specs=(hbm,) * 6,
        scratch_shapes=scratch,
        compiler_params=pltpu.CompilerParams(
            collective_id=0, has_side_effects=True, vmem_limit_bytes=26 * 1024 * 1024
        ),
    )(*[pltpu.with_memory_space_constraint(v, pltpu.HBM) for v in (act, sto, grd, gain, w, left, right)])
    return pl.pallas_call(
        finish_kernel,
        out_shape=(
            jax.ShapeDtypeStruct((128, 2048), BF16),
            jax.ShapeDtypeStruct((128, 2048), BF16),
            jax.ShapeDtypeStruct((16, 4, 512), F32),
            jax.ShapeDtypeStruct((1, 2048), F32),
            jax.ShapeDtypeStruct((2, 64, 64), F32),
            jax.ShapeDtypeStruct((2, 64, 64), F32),
        ),
        in_specs=[hbm] * 2 + [vmem] * 4,
        out_specs=(pl.BlockSpec(memory_space=pltpu.HBM),) * 2 + (vmem,) * 4,
        scratch_shapes=[pltpu.SemaphoreType.DMA((2,))],
        compiler_params=pltpu.CompilerParams(vmem_limit_bytes=8 * 1024 * 1024),
    )(*raw)


def shards(n_pipe, act_in, saved_in, grad_in, gain, weight, left_blocks, right_blocks):
    outs = section(n_pipe, act_in[0], saved_in[0], grad_in[0], gain, weight[0], left_blocks[0], right_blocks[0])
    handed, gradh, gw, gg, gl, gr = outs
    return (handed[None], gradh[None], gw[None], gg, gl[None], gr[None])


def solution(mesh):
    return jax.shard_map(
        functools.partial(shards, mesh.shape["pipe"]),
        mesh=mesh,
        in_specs=(
            P("pipe", "seq", None),
            P("pipe", "seq", None),
            P("pipe", "seq", None),
            P("pipe", None),
            P("pipe", "seq", None, None),
            P("pipe", "seq", None, None),
            P("pipe", "seq", None, None),
        ),
        out_specs=(
            P("pipe", "seq", None),
            P("pipe", "seq", None),
            P("pipe", "seq", None, None),
            P("pipe", None),
            P("pipe", "seq", None, None),
            P("pipe", "seq", None, None),
        ),
        check_vma=False,
    )
```

```python
import functools

import jax
import jax.numpy as jnp
from jax import lax
from jax.experimental import pallas as pl
from jax.experimental.pallas import tpu as pltpu
from jax.sharding import PartitionSpec as P

MESH = pl.DeviceIdType.MESH
F32 = jnp.float32
BF16 = jnp.bfloat16

KINDS = (
    "w", "gain", "sto", "left", "right", "stat", "grad", "act", "weight", "fs", "am", "fc", "ms", "ms2", "af", "af2", "mc",
    "gw", "gg", "gr", "gl", "msum", "msum2", "gwx", "ggx", "out", "gx",
)
SEM = {name: i for i, name in enumerate(KINDS)}


HALVES = (("af", (0, 2)), ("af2", (1, 3)))
MIXED = ("ms", "ms2")


def dot(a, b):
    return lax.dot_general(a, b, (((1,), (0,)), ((), ())), preferred_element_type=F32)


def dot_t(a, b):
    return lax.dot_general(a, b, (((1,), (1,)), ((), ())), preferred_element_type=F32)


def kernel(
    n_pipe,
    act, sto, grd, gain, w, left, right,
    handed, gradh, gw_out, gg_out, gl_out, gr_out,
    act_v, sto_v, w_v, left_v, right_v, w4, lpk, rpk,
    xs, xg, xc, lg, rg, wk, wfull, wnat, gn, st, stg, inv_s,
    ni_s, ni_c, ni_t, tmp, tmp2, s_t, r_m, r_t, p_s, p_c,
    q_m, q_t, l_m, l_t,
    fs, am, fc, fsr, amr, fcr, ms, af, mc, msr, afr, mcr,
    ap, an, gm, gws, gwr, gwx, ggs, ggw, ggr, ggx, msum, msumr, glp, grp, outb, gxb,
    send_sem, recv_sem, token_sem, load_sem,
):
    loads = [
        pltpu.make_async_copy(src, dst, load_sem.at[i])
        for i, (src, dst) in enumerate(((w, w_v), (left, left_v), (right, right_v), (act, act_v), (sto, sto_v)))
    ]
    for load in loads:
        load.start()

    pipe = lax.axis_index("pipe")
    seq = lax.axis_index("seq")
    core = lax.rem(pipe, 2)
    chip = pipe - core
    x = lax.div(seq, 8)
    z = lax.rem(seq, 8)
    side = lax.rem(z, 2)
    k = lax.div(z, 2)
    half = 1 - core
    g = 2 * x + half
    job = chip + side

    def ring(p):
        return lax.rem(p + n_pipe, n_pipe)

    turn = [lax.rem(k + d, 4) for d in (2, 1, 3, 0)]
    order = [lax.rem(k + d, 4) for d in (2, 3, 1, 0)]

    def worker_of(section, j):
        odd = lax.rem(section, 2)
        return (section - odd + 1 - side, 8 * x + 2 * j + odd)

    def owner_in(section, j):
        return (section, 8 * x + 2 * j + half)

    k_peers = [lax.rem(k + d, 4) for d in (2, 1, 3)]
    g_peers = [lax.rem(g + d, 8) for d in (4, 5, 3, 6, 2, 7, 1)]

    def dev_k(j):
        return (pipe, 8 * x + 2 * j + side)

    def dev_g(j):
        return (chip + 1 - lax.rem(j, 2), 8 * lax.div(j, 2) + z)

    def send(kind, src, dst, dev, arrival=None):
        pltpu.make_async_remote_copy(
            src_ref=src, dst_ref=dst, send_sem=send_sem.at[SEM[kind]],
            recv_sem=recv_sem.at[SEM[kind]] if arrival is None else arrival,
            device_id=dev, device_id_type=MESH,
        ).start()

    def wait(sem, kind, ref):
        pltpu.make_async_copy(ref, ref, sem.at[SEM[kind]]).wait()

    def arrived(kind, ref):
        wait(recv_sem, kind, ref)

    def piece(which, j, ref):
        pltpu.make_async_copy(ref.at[j], ref.at[j], token_sem.at[which, j]).wait()

    met = [dev_k(j) for j in k_peers] + [dev_g(j) for j in g_peers]
    for d in (-1, 0, 1):
        met += [owner_in(ring(job + d), j) for j in range(4)]
        met += [worker_of(ring(pipe + d), j) for j in range(4)]
    barrier = pltpu.get_barrier_semaphore()
    for dev in met:
        pl.semaphore_signal(barrier, inc=1, device_id=dev, device_id_type=MESH)
    for load in loads[:3]:
        load.wait()
    for j in range(4):
        w4[j] = w_v[:, j, :]
    for src, dst in ((left_v, lpk), (right_v, rpk)):
        dst[:, 0:64] = src[0]
        dst[:, 64:128] = src[1]
    pl.semaphore_wait(barrier, len(met))

    def cols(j):
        if isinstance(j, int):
            return pl.ds(j * 512, 512)
        return pl.ds(pl.multiple_of(j * 512, 512), 512)

    def send_out(kind, src, dst, to, j):
        stays = jnp.logical_and(to == pipe, k == j)

        @pl.when(stays)
        def _():
            pltpu.make_async_copy(src.at[j], dst.at[:, cols(k)], recv_sem.at[SEM[kind]]).start()

        @pl.when(jnp.logical_not(stays))
        def _():
            send(kind, src.at[j], dst.at[:, cols(k)], owner_in(to, j))

    def sent_out(kind, src, to):
        @pl.when(to == pipe)
        def _():
            wait(send_sem, kind, src.at[pl.ds(0, 3)])

        @pl.when(to != pipe)
        def _():
            wait(send_sem, kind, src)

    for j in turn:
        send("w", w4.at[j], wk.at[k], worker_of(pipe, j))
    for j in turn:
        send("left", lpk, lg.at[k], worker_of(pipe, j))
        send("gain", gain.at[:, cols(j)], gn.at[k], worker_of(pipe, j))

    def inv_row(x_ref):
        v = x_ref[...].astype(F32)
        inv = lax.rsqrt(jnp.sum(v * v, axis=1, keepdims=True) * (1.0 / 2048) + 1e-06)
        return jnp.transpose(jnp.broadcast_to(inv, (128, 128)))[0:8]

    loads[3].wait()
    st[0:8, :] = inv_row(act_v)
    loads[4].wait()
    st[8:16, :] = inv_row(sto_v)
    for j in turn:
        send("stat", st, stg.at[k], worker_of(pipe, j))
    for j in turn:
        send("act", act.at[:, cols(j)], xc.at[k], worker_of(pipe, j), token_sem.at[0, k])

    def nat(n, l):
        return 16 * (n >> 1) + 4 * (l >> 1) + 2 * (n & 1) + (l & 1)

    def pick_q(r):
        return 64 * ((r >> 3) & 1) + nat(r >> 4, r & 7)

    def pick_s(r):
        return 64 * (r & 7) + nat(r >> 6, (r >> 3) & 7)

    def hot(cond):
        return jnp.where(cond, 1.0, 0.0).astype(BF16)

    def rows(t, n=128):
        if isinstance(t, int):
            return pl.ds(t * n, n)
        return pl.ds(pl.multiple_of(t * n, n), n)

    col = lax.broadcasted_iota(jnp.int32, (128, 512), 1)
    row0 = lax.broadcasted_iota(jnp.int32, (128, 512), 0)
    lane = lax.broadcasted_iota(jnp.int32, (128, 128), 1)
    line = lax.broadcasted_iota(jnp.int32, (128, 128), 0)

    arrived("w", wk)
    for j in g_peers:
        send("weight", wk, wfull.at[g], dev_g(j))
    wfull[g] = wk[...]

    q_m[...] = hot(lane == pick_q(line))
    q_t[...] = hot(line == pick_q(lane))

    @pl.loop(0, 4)
    def _(t):
        s_t[rows(t), :] = hot(row0 + t * 128 == pick_s(col))

    def column(row8):
        return jnp.transpose(jnp.broadcast_to(row8[0:1, :], (128, 128)))

    def matmul(dst, a, b):
        @pl.loop(0, 2)
        def _(t):
            dst[rows(t, 256), :] = dot(a[rows(t, 256), :], b()).astype(dst.dtype)

    def matmul8(dst, a, b):
        @pl.loop(0, 2)
        def _(t):
            dst[pl.ds(t * 4, 4)] = dot(a[rows(t, 256), :], b()).astype(BF16).reshape(4, 64, 512)

    def scatter8(kind, src, dst):
        for j in g_peers:
            send(kind, src.at[j], dst.at[g], dev_g(j))
        dst[g] = src[g]

    def slot(t):
        if isinstance(t, int):
            return pl.ds(t * 16, 16)
        return pl.ds(pl.multiple_of(t * 16, 16), 16)

    def scatter_slot(kind, src, dst, t, value):
        src[:, slot(t), :] = value.astype(BF16).reshape(8, 16, 512)
        for j in g_peers:
            send(kind, src.at[j, slot(t)], dst.at[g, slot(t)], dev_g(j))
        dst[g, slot(t), :] = src[g, slot(t), :]

    def scatter_half(kind, src, dst, pair):
        for j in g_peers:
            for t in pair:
                send(kind, src.at[j, slot(t)], dst.at[g, slot(t)], dev_g(j))

    def slot_rows(ref, t):
        return ref[:, slot(t), :].reshape(128, 512)

    def flat(ref):
        return lambda: ref[...].reshape(512, 512)

    arrived("left", lg)

    @pl.loop(0, 4)
    def _(t):
        pair = lg[t].astype(F32)
        both = jnp.where((line >> 6) == (lane >> 6), jnp.concatenate([pair, pair], axis=0), 0.0)
        mixer = dot(q_m[...], both.astype(BF16))
        l_m[t] = mixer.astype(BF16)
        l_t[t] = jnp.transpose(mixer).astype(BF16)

    for j in turn:
        send("right", rpk, rg.at[k], worker_of(pipe, j))
    for j in turn:
        send("sto", sto.at[:, cols(j)], xs.at[k], worker_of(pipe, j), token_sem.at[1, k])
    arrived("weight", wfull.at[pl.ds(0, 7)])
    for n in range(8):
        for j in range(4):
            i = 16 * (8 * (n // 2) + 2 * j + n % 2)
            wnat[i:i + 16, :] = wfull[n, j]

    arrived("gain", gn)
    gain_k = gn[0]
    arrived("stat", stg)
    for t in order:
        piece(0, t, xc)
        inv = column(stg[t, 0:8, :])
        normed = xc[t].astype(F32) * inv[:, 0:1]
        ni_c[rows(t), :] = (normed * gain_k).astype(BF16)
        p_c[rows(t), :] = dot(ni_c[rows(t), :], wnat[...]).astype(BF16)
        scatter_slot("fc", fc, fcr, t, dot(l_m[t], p_c[rows(t), :]))

    for j in turn:
        send("grad", grd.at[:, cols(j)], xg.at[k], worker_of(pipe, j), token_sem.at[2, k])

    arrived("right", rg)

    @pl.loop(0, 4)
    def _(t):
        for i in range(2):
            pick = hot((row0 == 64 * i + (pick_s(col) & 63)) & ((col & 7) == 2 * t + i))
            tmp[pl.ds(pl.multiple_of(t * 128 + i * 64, 64), 64), :] = dot(rg[t], pick).astype(BF16)

    @pl.loop(0, 4)
    def _(t):
        r_m[rows(t), :] = dot(hot(col == pick_s(row0 + t * 128)), tmp[...]).astype(BF16)

    def transposed(dst, src):
        for t in range(4):
            dst[:, t * 128:(t + 1) * 128] = jnp.transpose(src[t * 128:(t + 1) * 128, :].astype(F32)).astype(BF16)

    arrived("fc", fcr.at[pl.ds(0, 7)])
    matmul8(mc, r_m, flat(fcr))
    scatter8("mc", mc, mcr)
    transposed(r_t, r_m)

    for t in order:
        piece(1, t, xs)
        inv = column(stg[t, 8:16, :])
        inv_s[t] = inv
        normed = xs[t].astype(F32) * inv[:, 0:1]
        ni_s[rows(t), :] = (normed * gain_k).astype(BF16)
        p_s[rows(t), :] = dot(ni_s[rows(t), :], wnat[...]).astype(BF16)
        scatter_slot("fs", fs, fsr, t, dot(l_m[t], p_s[rows(t), :]))
    transposed(ni_t, ni_s)

    for t in order:
        piece(2, t, xg)
        adj = (xg[t].astype(F32) * p_s[rows(t), :].astype(F32)).astype(BF16)
        scatter_slot("am", am, amr, t, dot(q_m[...], adj))

    arrived("mc", mcr.at[pl.ds(0, 7)])

    @pl.loop(0, 4)
    def _(t):
        mixed = dot(q_t[...], slot_rows(mcr, t))
        outb[t] = (xc[t].astype(F32) + p_c[rows(t), :].astype(F32) * mixed).astype(BF16)

    for j in (0, 2, 1, 3):
        send_out("out", outb, handed, ring(job + 1), j)

    arrived("fs", fsr.at[pl.ds(0, 7)])
    matmul8(ms, r_m, flat(fsr))
    scatter_half("ms", ms, msr, HALVES[0][1])
    arrived("am", amr.at[pl.ds(0, 7)])
    matmul8(af, r_t, flat(amr))
    scatter_half("af", af, afr, HALVES[0][1])
    scatter_half("ms2", ms, msr, HALVES[1][1])
    scatter_half("af2", af, afr, HALVES[1][1])
    msr[g] = ms[g]
    afr[g] = af[g]

    matmul(tmp2, s_t, flat(fsr))
    matmul(tmp, s_t, flat(amr))

    @pl.loop(0, 4)
    def _(t):
        for i in range(2):
            part = pl.ds(pl.multiple_of(t * 128 + i * 64, 64), 64)
            grp[t, :, i * 64:(i + 1) * 64] = dot_t(tmp[part, :], tmp2[part, :]).astype(BF16)

    for j in turn:
        send("gr", grp.at[j], gr_out.at[k], owner_in(job, j))

    ggs[...] = jnp.zeros((8, 512), F32)

    def adjoint_proj(h):
        kind, pair = HALVES[h]
        arrived(MIXED[h], msr.at[pl.ds(0, 7), pl.ds(0, 32)])
        for t in pair:
            gm[rows(t), :] = xg[t].astype(F32) * dot(q_t[...], slot_rows(msr, t))
        arrived(kind, afr.at[pl.ds(0, 7), pl.ds(0, 32)])
        sums = []
        for t in pair:
            adj = (gm[rows(t), :] + dot(l_t[t], slot_rows(afr, t))).astype(BF16)
            ap[rows(t), :] = adj
            part = jnp.sum(adj.astype(F32) * p_s[rows(t), :].astype(F32), axis=1, keepdims=True)
            sums.append(jnp.transpose(jnp.broadcast_to(part, (128, 128)))[0:4])
        msum[h] = jnp.concatenate(sums, axis=0)
        for j in k_peers:
            send("msum2" if h else "msum", msum.at[h], msumr.at[h, k], dev_k(j))
        msumr[h, k] = msum[h]

    def adjoint_norm(h):
        for t in HALVES[h][1]:
            adj_norm = dot_t(ap[rows(t), :], wnat[...])
            inv = inv_s[t, :, 0:1]
            normed = xs[t].astype(F32) * inv
            an[rows(t), :] = xg[t].astype(F32) + inv * (adj_norm * gain_k)
            ggs[...] += jnp.sum((adj_norm * normed).reshape(16, 8, 512), axis=0)

    def input_grad(h):
        arrived("msum2" if h else "msum", msumr.at[h, pl.ds(0, 3)])
        total = msumr[h, 0] + msumr[h, 1] + msumr[h, 2] + msumr[h, 3]
        for n, t in enumerate(HALVES[h][1]):
            inv = inv_s[t]
            weight = (inv * inv * column(total[4 * n:4 * n + 4]))[:, 0:1] * (1.0 / 2048)
            gxb[t] = (an[rows(t), :] - xs[t].astype(F32) * weight).astype(BF16)
            send_out("gx", gxb, gradh, ring(job - 1), t)

    adjoint_proj(0)
    adjoint_norm(0)
    adjoint_proj(1)
    input_grad(0)

    @pl.loop(0, 4)
    def _(t):
        gws[t] = dot(ni_t[rows(t), :], ap[...]).astype(BF16).reshape(4, 2, 16, 512)

    for j in g_peers:
        send("gw", gws.at[lax.div(j, 2), :, lax.rem(j, 2)], gwr.at[g], dev_g(j))
    gwr[g] = gws[lax.div(g, 2), :, lax.rem(g, 2)]
    adjoint_norm(1)

    @pl.loop(0, 4)
    def _(t):
        tmp[rows(t), :] = dot(q_t[...], slot_rows(afr, t)).astype(BF16)
        for i in range(2):
            part = pl.ds(pl.multiple_of(t * 128 + i * 64, 64), 64)
            glp[t, :, i * 64:(i + 1) * 64] = dot_t(tmp[part, :], p_s[part, :]).astype(BF16)

    for j in turn:
        send("gl", glp.at[j], gl_out.at[k], owner_in(job, j))

    ggw[...] = jnp.sum(ggs[...], axis=0, keepdims=True)
    for j in g_peers:
        send("gg", ggw, ggr.at[g], dev_g(j))
    ggr[g] = ggw[...]
    input_grad(1)

    arrived("gg", ggr.at[pl.ds(0, 7)])
    summed = ggr[0]
    for j in range(1, 8):
        summed = summed + ggr[j]
    ggx[...] = summed
    for j in turn:
        send("ggx", ggx, gg_out.at[k], owner_in(job, j))
    arrived("gw", gwr.at[pl.ds(0, 7)])
    for t in range(4):
        acc = gwr[0, t].astype(F32)
        for j in range(1, 8):
            acc = acc + gwr[j, t].astype(F32)
        gwx[t] = acc.astype(BF16)
    for j in turn:
        send("gwx", gwx.at[j], gw_out.at[k], owner_in(job, j))

    arrived("gr", gr_out)
    arrived("gl", gl_out)
    arrived("ggx", gg_out)
    arrived("gwx", gw_out)
    arrived("gx", gradh)
    arrived("out", handed)

    for kind, ref in (
        ("w", wk),
        ("gain", gn),
        ("sto", xs),
        ("left", lg),
        ("right", rg),
        ("stat", stg),
        ("grad", xg),
        ("act", xc),
        ("weight", wfull.at[pl.ds(0, 7)]),
        ("fs", fsr.at[pl.ds(0, 7)]),
        ("am", amr.at[pl.ds(0, 7)]),
        ("fc", fcr.at[pl.ds(0, 7)]),
        ("ms", msr.at[pl.ds(0, 7), pl.ds(0, 32)]),
        ("ms2", msr.at[pl.ds(0, 7), pl.ds(0, 32)]),
        ("af", afr.at[pl.ds(0, 7), pl.ds(0, 32)]),
        ("af2", afr.at[pl.ds(0, 7), pl.ds(0, 32)]),
        ("mc", mcr.at[pl.ds(0, 7)]),
        ("gw", gwr.at[pl.ds(0, 7)]),
        ("gg", ggr.at[pl.ds(0, 7)]),
        ("gr", grp),
        ("gl", glp),
        ("msum", msumr.at[0, pl.ds(0, 3)]),
        ("msum2", msumr.at[1, pl.ds(0, 3)]),
        ("gwx", gwx),
        ("ggx", gg_out),
    ):
        wait(send_sem, kind, ref)
    sent_out("out", outb, ring(job + 1))
    sent_out("gx", gxb, ring(job - 1))


def finish_kernel(handed, gradh, gw, gg, gl, gr, handed_o, gradh_o, gw_o, gg_o, gl_o, gr_o, sems):
    copies = [
        pltpu.make_async_copy(handed, handed_o, sems.at[0]),
        pltpu.make_async_copy(gradh, gradh_o, sems.at[1]),
    ]
    for copy in copies:
        copy.start()
    for j in range(4):
        gw_o[:, j, :] = gw[j].astype(F32)
        gg_o[0:1, j * 512:(j + 1) * 512] = gg[j]
    for src, dst in ((gl, gl_o), (gr, gr_o)):
        total = src[0].astype(F32) + src[1].astype(F32) + src[2].astype(F32) + src[3].astype(F32)
        dst[0] = total[:, 0:64]
        dst[1] = total[:, 64:128]
    for copy in copies:
        copy.wait()


def section(n_pipe, act, sto, grd, gain, w, left, right):
    vmem = pl.BlockSpec(memory_space=pltpu.VMEM)
    hbm = pl.BlockSpec(memory_space=pl.ANY)
    rows_all = pltpu.VMEM((128, 2048), BF16)
    big = pltpu.VMEM((512, 512), BF16)
    parts = pltpu.VMEM((8, 64, 512), BF16)
    tokens = pltpu.VMEM((4, 128, 512), BF16)
    pair = pltpu.VMEM((64, 128), BF16)
    pairs = pltpu.VMEM((4, 64, 128), BF16)
    square = pltpu.VMEM((128, 128), BF16)
    squares = pltpu.VMEM((4, 128, 128), BF16)
    scratch = (
        [rows_all] * 2
        + [pltpu.VMEM((16, 4, 512), BF16), pltpu.VMEM((2, 64, 64), BF16), pltpu.VMEM((2, 64, 64), BF16)]
        + [pltpu.VMEM((4, 16, 512), BF16), pair, pair]
        + [tokens] * 3
        + [pairs] * 2
        + [pltpu.VMEM((4, 16, 512), BF16), pltpu.VMEM((8, 4, 16, 512), BF16), big, pltpu.VMEM((4, 1, 512), F32)]
        + [pltpu.VMEM((16, 128), F32), pltpu.VMEM((4, 16, 128), F32), pltpu.VMEM((4, 128, 128), F32)]
        + [big] * 10
        + [square, square, squares, squares]
        + [parts] * 12
        + [big, pltpu.VMEM((512, 512), F32), pltpu.VMEM((512, 512), F32)]
        + [pltpu.VMEM((4, 4, 2, 16, 512), BF16), pltpu.VMEM((8, 4, 16, 512), BF16), pltpu.VMEM((4, 16, 512), BF16)]
        + [pltpu.VMEM((8, 512), F32), pltpu.VMEM((1, 512), F32), pltpu.VMEM((8, 1, 512), F32), pltpu.VMEM((1, 512), F32)]
        + [pltpu.VMEM((2, 8, 128), F32), pltpu.VMEM((2, 4, 8, 128), F32)]
        + [pairs] * 2
        + [tokens] * 2
        + [pltpu.SemaphoreType.DMA((len(KINDS),)), pltpu.SemaphoreType.DMA((len(KINDS),))]
        + [pltpu.SemaphoreType.DMA((3, 4)), pltpu.SemaphoreType.DMA((5,))]
    )
    raw = pl.pallas_call(
        functools.partial(kernel, n_pipe),
        out_shape=(
            jax.ShapeDtypeStruct((128, 2048), BF16),
            jax.ShapeDtypeStruct((128, 2048), BF16),
            jax.ShapeDtypeStruct((4, 16, 512), BF16),
            jax.ShapeDtypeStruct((4, 1, 512), F32),
            jax.ShapeDtypeStruct((4, 64, 128), BF16),
            jax.ShapeDtypeStruct((4, 64, 128), BF16),
        ),
        in_specs=[pl.BlockSpec(memory_space=pltpu.HBM)] * 7,
        out_specs=(hbm,) * 6,
        scratch_shapes=scratch,
        compiler_params=pltpu.CompilerParams(
            collective_id=0, has_side_effects=True, vmem_limit_bytes=26 * 1024 * 1024
        ),
    )(*[pltpu.with_memory_space_constraint(v, pltpu.HBM) for v in (act, sto, grd, gain, w, left, right)])
    return pl.pallas_call(
        finish_kernel,
        out_shape=(
            jax.ShapeDtypeStruct((128, 2048), BF16),
            jax.ShapeDtypeStruct((128, 2048), BF16),
            jax.ShapeDtypeStruct((16, 4, 512), F32),
            jax.ShapeDtypeStruct((1, 2048), F32),
            jax.ShapeDtypeStruct((2, 64, 64), F32),
            jax.ShapeDtypeStruct((2, 64, 64), F32),
        ),
        in_specs=[hbm] * 2 + [vmem] * 4,
        out_specs=(pl.BlockSpec(memory_space=pltpu.HBM),) * 2 + (vmem,) * 4,
        scratch_shapes=[pltpu.SemaphoreType.DMA((2,))],
        compiler_params=pltpu.CompilerParams(vmem_limit_bytes=8 * 1024 * 1024),
    )(*raw)


def shards(n_pipe, act_in, saved_in, grad_in, gain, weight, left_blocks, right_blocks):
    outs = section(n_pipe, act_in[0], saved_in[0], grad_in[0], gain, weight[0], left_blocks[0], right_blocks[0])
    handed, gradh, gw, gg, gl, gr = outs
    return (handed[None], gradh[None], gw[None], gg, gl[None], gr[None])


def solution(mesh):
    return jax.shard_map(
        functools.partial(shards, mesh.shape["pipe"]),
        mesh=mesh,
        in_specs=(
            P("pipe", "seq", None),
            P("pipe", "seq", None),
            P("pipe", "seq", None),
            P("pipe", None),
            P("pipe", "seq", None, None),
            P("pipe", "seq", None, None),
            P("pipe", "seq", None, None),
        ),
        out_specs=(
            P("pipe", "seq", None),
            P("pipe", "seq", None),
            P("pipe", "seq", None, None),
            P("pipe", None),
            P("pipe", "seq", None, None),
            P("pipe", "seq", None, None),
        ),
        check_vma=False,
    )
```
